512 devices in a mesh: gx: 32 (over x, y, core), gy: 16 (over z).
Axes of the slice: x: 4, y: 4, z: 16, core: 2. Of those that a mesh axis runs over, the one named last changes fastest.
Arguments:
- hidden_states: bfloat16 [16, 256, 2048], P('gy', 'gx'), may hold values from -500 to 500
- norm_gain: float32 [2048], replicated, may hold values from 0.1 to 1.9
- norm_bias: float32 [2048], replicated, may hold values from -3 to 3
- query_weight: bfloat16 [2048, 2048], P('gy', 'gx'), may hold values from -0.125 to 0.125
- keyvalue_weight: bfloat16 [2048, 256], P('gy', 'gx'), may hold values from -0.125 to 0.125
- out_weight: bfloat16 [2048, 2048], P('gx', 'gy'), may hold values from -0.75 to 0.75
- key_cache: bfloat16 [16, 2304, 128], P('gy', 'gx'), may hold values from -400 to 400
- value_cache: bfloat16 [16, 2304, 128], P('gy', 'gx'), may hold values from -6 to 6
- cache_length: int32 [16], P('gy'), may hold values from 0 to 2048, as said below
Outputs:
- attention_out: bfloat16 [16, 256, 2048], P('gy', 'gx')
- new_key_cache: bfloat16 [16, 2304, 128], P('gy', 'gx')
- new_value_cache: bfloat16 [16, 2304, 128], P('gy', 'gx')
The draws below stay inside these ranges and needn't reach their ends.
Inputs may be any that keep to these rules, and one draw needn't show every extreme that they name: Request r holds cache_length[r] earlier tokens; its new tokens take positions cache_length[r] to cache_length[r] + 255. Some request holds exactly 2048.
All inputs are finite; a program needn't handle non-finite values.
Results may differ from the reference program's by a relative error of at most 0.012.
The reference program's roundings to bfloat16 on the way count: a program that leaves them out, or rounds other values in their place, can miss the bound.
Values may be sent and summed in bfloat16 or wider, within the bound.
No kernel may reach another device: no remote copies, remote signals or barrier semaphores. Data moves between devices by JAX's collectives and lax.ppermute only.
A program may use at most 192 MiB of HBM per device.

```python
import math
import jax
import jax.numpy as jnp
from jax import lax

D = 2048
HEADS = 16
HEAD_DIM = 128
NEW_TOK = 256
CACHE_MAX = 2048
REQUESTS = 16
SEQ_CAP = 2304
PAGE = 72


def draw_hidden_states(key, part):
    key_rows, key_cols, key_base = jax.random.split(key, 3)
    full_shape = (REQUESTS, NEW_TOK, D)
    row_scale = jnp.exp(jax.random.uniform(key_rows, (REQUESTS, NEW_TOK, 1), jnp.float32, 0.0, math.log(10.0)))
    col_scale = jnp.exp(jax.random.uniform(key_cols, (1, 1, D), jnp.float32, 0.0, math.log(10.0)))
    entries = jnp.clip(jax.random.normal(key_base, full_shape, jnp.float32), -5.0, 5.0)
    return (entries * row_scale * col_scale).astype(jnp.bfloat16)


def draw_key_cache(key, part):
    key_base = jax.random.fold_in(key, 0)
    full_shape = (REQUESTS, SEQ_CAP, HEAD_DIM)
    entries = 2.0 * jnp.clip(jax.random.normal(key_base, full_shape, jnp.float32), -5.0, 5.0)
    return entries.astype(jnp.bfloat16)


def draw_cache_length(key, part):
    key_len, key_pick = jax.random.split(key, 2)
    lengths = jax.random.randint(key_len, (REQUESTS,), 0, CACHE_MAX + 1, dtype=jnp.int32)
    chosen = jax.random.randint(key_pick, (), 0, REQUESTS, dtype=jnp.int32)
    return jnp.where(jnp.arange(REQUESTS, dtype=jnp.int32) == chosen, CACHE_MAX, lengths).astype(jnp.int32)


def levels(key, shape, cuts, least, high):
    def one(axis_at, parts):
        steps = jax.random.uniform(jax.random.fold_in(jax.random.fold_in(key, 6), axis_at), (parts,), jnp.float32, least / len(cuts), high / len(cuts))
        return jnp.repeat(jnp.exp(steps), shape[axis_at] // parts).reshape((-1,) + (1,) * (len(shape) - axis_at - 1))

    factor_of = one(*cuts[0])
    for cut in cuts[1:]:
        factor_of = factor_of * one(*cut)
    return factor_of


def bell_draw(stream_key, extent, deviation, most, cuts=(), held_as=jnp.bfloat16):
    values = deviation * jax.random.normal(stream_key, extent, jnp.float32)
    if cuts:
        values = values * levels(stream_key, extent, cuts, -0.22, 0.18)
    return jnp.clip(values, -most, most).astype(held_as)


def setup_inputs(seed: int = 0) -> dict:
    splits = jax.random.split(jax.random.key(seed), 10)
    return {
        "hidden_states": draw_hidden_states(jax.random.fold_in(splits[9], 71), 0),
        "norm_gain": jnp.clip(1.0 + 0.18 * jax.random.normal(splits[1], (D,), jnp.float32), 0.1, 1.9),
        "norm_bias": bell_draw(splits[2], (D,), 0.5, 3.0, (), jnp.float32),
        "query_weight": bell_draw(splits[3], (D, HEADS * HEAD_DIM), D ** -0.5, 0.125, ((0, 16), (1, 32))),
        "keyvalue_weight": bell_draw(splits[4], (D, 2 * HEAD_DIM), D ** -0.5, 0.125, ((0, 16), (1, 32))),
        "out_weight": bell_draw(splits[5], (HEADS * HEAD_DIM, D), (HEADS * HEAD_DIM // 32) ** -0.5, 0.75, ((0, 32), (1, 16))),
        "key_cache": draw_key_cache(jax.random.fold_in(splits[9], 71), 0),
        "value_cache": bell_draw(splits[7], (REQUESTS, SEQ_CAP, HEAD_DIM), 1.0, 6.0, ((0, 16), (1, 32))),
        "cache_length": draw_cache_length(jax.random.fold_in(splits[9], 71), 0),
    }


NEGATIVE = -1e+30

def normalize(hidden_states, norm_gain, norm_bias):
    values = hidden_states.astype(jnp.float32)
    average = lax.optimization_barrier(jnp.mean(values, axis=-1, keepdims=True))
    centred = values - average
    spread = lax.optimization_barrier(jnp.mean(centred * centred, axis=-1, keepdims=True))
    return (centred * lax.rsqrt(spread + 1e-05) * norm_gain + norm_bias).astype(jnp.bfloat16)

def page_terms(query_rows, query_pos, key_rows, value_rows, first_pos, page_size):
    row_count = query_rows.shape[0]
    head_dim = key_rows.shape[1]
    page_count = key_rows.shape[0] // page_size
    scores = jnp.dot(query_rows, key_rows.T, preferred_element_type=jnp.float32)
    scores = (scores * head_dim ** (-0.5)).reshape(row_count, page_count, page_size)
    key_pos = first_pos + jnp.arange(page_count * page_size, dtype=jnp.int32).reshape(page_count, page_size)
    allowed = key_pos[None, :, :] <= query_pos[:, None, None]
    maxima = lax.optimization_barrier(jnp.max(jnp.where(allowed, scores, NEGATIVE), axis=2))
    weights = jnp.where(allowed, jnp.exp(scores - maxima[:, :, None]), 0.0)
    totals = lax.optimization_barrier(jnp.sum(weights, axis=2))
    rounded = lax.optimization_barrier(weights.astype(jnp.bfloat16))
    weighted = jnp.einsum('rnp,npd->rnd', rounded.astype(jnp.float32), value_rows.reshape(page_count, page_size, head_dim).astype(jnp.float32))
    return (maxima, totals, weighted)

def reduce_pages(maxima, totals, weighted):
    largest = lax.optimization_barrier(jnp.max(maxima, axis=1))
    factor = jnp.exp(maxima - largest[:, None])
    return (largest, lax.optimization_barrier(jnp.sum(totals * factor, axis=1)), lax.optimization_barrier(jnp.sum(weighted * factor[:, :, None], axis=1)))

def pick_rows(rows_keyvalue, indices):
    return jnp.take(rows_keyvalue, indices, axis=0)

def reference(hidden_states, norm_gain, norm_bias, query_weight, keyvalue_weight, out_weight, key_cache, value_cache, cache_length):
    normed = normalize(hidden_states, norm_gain, norm_bias).reshape(REQUESTS * NEW_TOK, D)
    queries = jnp.dot(normed, query_weight, preferred_element_type=jnp.float32).astype(jnp.bfloat16)
    queries = queries.reshape(REQUESTS, NEW_TOK, HEADS * HEAD_DIM)
    keyvalue = jnp.dot(normed, keyvalue_weight, preferred_element_type=jnp.float32).astype(jnp.bfloat16)
    keyvalue = keyvalue.reshape(REQUESTS, NEW_TOK, 2 * HEAD_DIM)
    offsets = jnp.arange(SEQ_CAP, dtype=jnp.int32)[None, :] - cache_length.astype(jnp.int32)[:, None]
    inside = (offsets >= 0) & (offsets < NEW_TOK)
    picked = jax.vmap(pick_rows)(keyvalue, jnp.clip(offsets, 0, NEW_TOK - 1).astype(jnp.int32))
    new_key_cache = jnp.where(inside[:, :, None], picked[:, :, :HEAD_DIM], key_cache)
    new_value_cache = jnp.where(inside[:, :, None], picked[:, :, HEAD_DIM:], value_cache)
    row_total = NEW_TOK * HEADS
    row_block = math.gcd(row_total, 512)

    def one_request(packed):
        query_all, key_rows, value_rows, length = packed
        rows_all = query_all.reshape(row_total // row_block, row_block, HEAD_DIM)
        row_pos = (length + jnp.arange(row_total, dtype=jnp.int32) // HEADS).reshape(row_total // row_block, row_block)

        def one_block(block_args):
            maxima, totals, weighted = page_terms(block_args[0], block_args[1], key_rows, value_rows, jnp.int32(0), PAGE)
            largest, weight_sum, summed = reduce_pages(maxima, totals, weighted)
            return summed / weight_sum[:, None]
        result = lax.map(one_block, (rows_all, row_pos))
        return result.reshape(NEW_TOK, HEADS * HEAD_DIM).astype(jnp.bfloat16)
    attended = lax.map(one_request, (queries, new_key_cache, new_value_cache, cache_length.astype(jnp.int32)))
    attention_out = jnp.dot(attended.reshape(REQUESTS * NEW_TOK, HEADS * HEAD_DIM), out_weight, preferred_element_type=jnp.float32).astype(jnp.bfloat16)
    return (attention_out.reshape(REQUESTS, NEW_TOK, D), new_key_cache, new_value_cache)
```

```python
import jax
import jax.numpy as jnp
from jax import lax
from jax.experimental import pallas as pl
from jax.experimental.pallas import tpu as pltpu
from jax.sharding import PartitionSpec as P

CHIPS = 16
CORES = 2
LANES = 128
HALF = 64
PAGE = 72
OWN = 8
FEATURES = 2048
CHUNKS = FEATURES // LANES
KV_ROWS = 2 * PAGE
SEND_ROWS = KV_ROWS + OWN * CHUNKS
WEIGHT_ROWS = HALF + OWN
NEW = 256
NEGATIVE = -1e30

SAME_CORE = [[CORES * chip + core for chip in range(CHIPS)] for core in range(CORES)]
ONE_CHIP = [[CORES * chip + core for core in range(CORES)] for chip in range(CHIPS)]
SWAP = [(place, place ^ 1) for place in range(CHIPS * CORES)]

F32 = jnp.float32
BF16 = jnp.bfloat16


def dot(a, b):
    return lax.dot_general(a, b, (((1,), (0,)), ((), ())), preferred_element_type=F32)


def dot_nt(a, b):
    return lax.dot_general(a, b, (((1,), (1,)), ((), ())), preferred_element_type=F32)


def iota(shape, dim):
    return lax.broadcasted_iota(jnp.int32, shape, dim)


def eye(rows, columns, shift):
    return (iota((rows, columns), 0) + shift == iota((rows, columns), 1)).astype(F32).astype(BF16)


def prepare(hidden, gain, bias, query_w, keyvalue_w, out_w, key_page, value_page, send, weights):
    values = hidden[...].astype(F32)
    average = jnp.mean(values, axis=-1, keepdims=True)
    centred = values - average
    spread = jnp.mean(centred * centred, axis=-1, keepdims=True)
    normed = (centred * lax.rsqrt(spread + 1e-05) * gain[...] + bias[...]).astype(BF16)
    key_rows = key_page[...]
    value_rows = value_page[...]
    for chip in range(CHIPS):
        send[chip, 0:PAGE, :] = key_rows
        send[chip, PAGE:KV_ROWS, :] = value_rows
        for chunk in range(CHUNKS):
            send[chip, KV_ROWS + OWN * chunk : KV_ROWS + OWN * (chunk + 1), :] = normed[
                :, LANES * chunk : LANES * (chunk + 1)
            ]
    packed = dot(query_w[0:HALF, :], eye(HALF, LANES, 0)) + dot(query_w[HALF:LANES, :], eye(HALF, LANES, HALF))
    weights[0:HALF, :] = packed.astype(BF16)
    weights[HALF:WEIGHT_ROWS, :] = dot_nt(eye(OWN, OWN, 0), keyvalue_w[...]).astype(BF16)
    weights[WEIGHT_ROWS : WEIGHT_ROWS + HALF, :] = out_w[...]


def project(tokens, weights, queries, keyvalue):
    low = iota((HALF, LANES), 1) < HALF
    query_sum = jnp.zeros((LANES, LANES), F32)
    keyvalue_sum = jnp.zeros((CORES * OWN, LANES), F32)
    for chunk in range(CHUNKS):
        first = KV_ROWS + OWN * chunk
        rows = tokens[:, first : first + OWN, :].astype(F32).reshape(LANES, LANES).astype(BF16)
        left = weights[0, chunk, 0:HALF, :].astype(F32)
        right = weights[1, chunk, 0:HALF, :].astype(F32)
        upper = jnp.where(low, left, pltpu.roll(right, HALF, 1))
        lower = jnp.where(low, pltpu.roll(left, HALF, 1), right)
        square = jnp.concatenate([upper, lower], axis=0).astype(BF16)
        query_sum = query_sum + dot(rows, square)
        narrow = jnp.concatenate(
            [
                weights[0, chunk, HALF:WEIGHT_ROWS, :].astype(F32),
                weights[1, chunk, HALF:WEIGHT_ROWS, :].astype(F32),
            ],
            axis=0,
        ).astype(BF16)
        keyvalue_sum = keyvalue_sum + dot_nt(narrow, rows)
    queries[...] = query_sum.astype(BF16)
    rounded = keyvalue_sum.astype(BF16)
    for place in range(CHIPS * CORES):
        keyvalue[place] = rounded


def new_columns(keyvalue, core, first):
    return jnp.concatenate([keyvalue[CORES * chip + core] for chip in range(first, first + CHIPS // 2)], axis=0)


def token_of(index, core):
    return ((index >> 3) << 4) + OWN * core + (index & 7)


def attend(length_ref, core_ref, queries, own, peer, keyvalue, out_w, result):
    length = length_ref[0]
    core = core_ref[0]
    scale = float(LANES) ** (-0.5)
    query_rows = queries[...]
    places = CHIPS * PAGE
    lane = iota((1, places), 1)
    start = lane + PAGE * ((lane * 911) >> 16)
    scored = []
    value_sets = []
    for source, side in ((own, core), (peer, 1 - core)):
        keys = source[:, 0:PAGE, :].astype(F32).reshape(places, LANES).astype(BF16)
        value_sets.append(source[:, PAGE:KV_ROWS, :].astype(F32).reshape(places, LANES).astype(BF16))
        scores = dot_nt(query_rows, keys) * scale
        scored.append(jnp.where(start + PAGE * side < length, scores, NEGATIVE))
    own_token = token_of(iota((LANES, LANES), 0), core)
    for side in range(CORES):
        scores = dot(query_rows, new_columns(keyvalue, side, 0)) * scale
        scored.append(jnp.where(token_of(iota((LANES, LANES), 1), side) <= own_token, scores, NEGATIVE))
    largest = jnp.max(scored[0], axis=1, keepdims=True)
    for scores in scored[1:]:
        largest = jnp.maximum(largest, jnp.max(scores, axis=1, keepdims=True))
    total = jnp.zeros((LANES, 1), F32)
    summed = jnp.zeros((LANES, LANES), F32)
    for which, scores in enumerate(scored):
        terms = jnp.exp(scores - largest)
        total = total + jnp.sum(terms, axis=1, keepdims=True)
        if which < 2:
            summed = summed + dot(terms.astype(BF16), value_sets[which])
        else:
            summed = summed + dot_nt(terms.astype(BF16), new_columns(keyvalue, which - 2, CHIPS // 2))
    attended = (summed / total).astype(BF16)
    for chunk in range(CHUNKS):
        square = jnp.concatenate([out_w[0, chunk], out_w[1, chunk]], axis=0)
        part = dot(attended, square)
        result[:, OWN * chunk : OWN * (chunk + 1), :] = part.reshape(CHIPS, OWN, LANES)


def add_heads(parts, result):
    total = parts[0]
    for chip in range(1, CHIPS):
        total = total + parts[chip]
    for chunk in range(CHUNKS):
        result[:, LANES * chunk : LANES * (chunk + 1)] = total[OWN * chunk : OWN * (chunk + 1), :].astype(BF16)


def write_pages(length_ref, place_ref, keyvalue, key_page, value_page, new_key, new_value):
    length = length_ref[0]
    base = place_ref[0] * PAGE - length
    offset = iota((PAGE, LANES), 0) + base
    inside = (offset >= 0) & (offset < NEW)
    key_rows = jnp.zeros((PAGE, LANES), F32)
    value_rows = jnp.zeros((PAGE, LANES), F32)
    for side in range(CORES):
        chosen = (offset == token_of(iota((PAGE, LANES), 1), side)).astype(F32).astype(BF16)
        key_rows = key_rows + dot_nt(chosen, new_columns(keyvalue, side, 0))
        value_rows = value_rows + dot_nt(chosen, new_columns(keyvalue, side, CHIPS // 2))
    new_key[...] = jnp.where(inside, key_rows, key_page[...].astype(F32)).astype(BF16)
    new_value[...] = jnp.where(inside, value_rows, value_page[...].astype(F32)).astype(BF16)


def call(kernel, shapes, arguments, scalars=0):
    specs = [
        pl.BlockSpec(memory_space=pltpu.SMEM if at < scalars else pltpu.VMEM) for at in range(len(arguments))
    ]
    return pl.pallas_call(
        kernel,
        out_shape=[jax.ShapeDtypeStruct(shape, dtype) for shape, dtype in shapes],
        in_specs=specs,
        out_specs=[pl.BlockSpec(memory_space=pltpu.VMEM)] * len(shapes),
        compiler_params=pltpu.CompilerParams(vmem_limit_bytes=48 * 1024 * 1024),
    )(*arguments)


def body(
    hidden_states,
    norm_gain,
    norm_bias,
    query_weight,
    keyvalue_weight,
    out_weight,
    key_cache,
    value_cache,
    cache_length,
):
    place = lax.axis_index("gx").astype(jnp.int32).reshape(1)
    core = place & 1
    send, weights = call(
        prepare,
        [((CHIPS, SEND_ROWS, LANES), BF16), ((WEIGHT_ROWS + HALF, LANES), BF16)],
        (
            hidden_states[0],
            norm_gain.reshape(1, FEATURES),
            norm_bias.reshape(1, FEATURES),
            query_weight,
            keyvalue_weight,
            out_weight,
            key_cache[0],
            value_cache[0],
        ),
    )
    own = lax.all_to_all(send, "gx", 0, 0, tiled=True, axis_index_groups=SAME_CORE)
    planes = lax.all_gather(weights, "gy", axis=0, tiled=False)
    inner = lax.all_gather(planes[:, :WEIGHT_ROWS], "gx", axis=0, tiled=False, axis_index_groups=ONE_CHIP)
    queries, rows = call(
        project,
        [((LANES, LANES), BF16), ((CHIPS * CORES, CORES * OWN, LANES), BF16)],
        (own, inner),
    )
    keyvalue = lax.all_to_all(rows, "gx", 0, 0, tiled=True)
    peer = lax.ppermute(own[:, :KV_ROWS], "gx", SWAP)
    outer = lax.all_gather(planes[:, WEIGHT_ROWS:], "gx", axis=0, tiled=False, axis_index_groups=ONE_CHIP)
    (parts,) = call(
        attend,
        [((CHIPS, LANES, LANES), F32)],
        (cache_length, core, queries, own, peer, keyvalue, outer),
        scalars=2,
    )
    collected = lax.all_to_all(parts, "gx", 0, 0, tiled=True, axis_index_groups=SAME_CORE)
    new_key, new_value = call(
        write_pages,
        [((PAGE, LANES), BF16), ((PAGE, LANES), BF16)],
        (cache_length, place, keyvalue, key_cache[0], value_cache[0]),
        scalars=2,
    )
    (out,) = call(add_heads, [((OWN, FEATURES), BF16)], (collected,))
    return (out[None], new_key[None], new_value[None])


def solution(mesh):
    return jax.shard_map(
        body,
        mesh=mesh,
        in_specs=(
            P("gy", "gx", None),
            P(),
            P(),
            P("gy", "gx"),
            P("gy", "gx"),
            P("gx", "gy"),
            P("gy", "gx", None),
            P("gy", "gx", None),
            P("gy"),
        ),
        out_specs=(P("gy", "gx", None), P("gy", "gx", None), P("gy", "gx", None)),
        check_vma=False,
    )
```

```python
import jax
import jax.numpy as jnp
from jax import lax
from jax.experimental import pallas as pl
from jax.experimental.pallas import tpu as pltpu
from jax.sharding import PartitionSpec as P

CHIPS = 16
CORES = 2
LANES = 128
HALF = 64
PAGE = 72
OWN = 8
FEATURES = 2048
CHUNKS = FEATURES // LANES
KV_ROWS = 2 * PAGE
SEND_ROWS = KV_ROWS + OWN * CHUNKS
WEIGHT_ROWS = HALF + OWN
NEW = 256
NEGATIVE = -1e30

SAME_CORE = [[CORES * chip + core for chip in range(CHIPS)] for core in range(CORES)]
ONE_CHIP = [[CORES * chip + core for core in range(CORES)] for chip in range(CHIPS)]
SWAP = [(place, place ^ 1) for place in range(CHIPS * CORES)]

F32 = jnp.float32
BF16 = jnp.bfloat16


def dot(a, b):
    return lax.dot_general(a, b, (((1,), (0,)), ((), ())), preferred_element_type=F32)


def dot_nt(a, b):
    return lax.dot_general(a, b, (((1,), (1,)), ((), ())), preferred_element_type=F32)


def iota(shape, dim):
    return lax.broadcasted_iota(jnp.int32, shape, dim)


def prepare(hidden, gain, bias, query_w, keyvalue_w, out_w, key_page, value_page, send, weights, *scratch):
    held, done = scratch[:-1], scratch[-1]
    targets = held + (
        weights.at[0:HALF],
        weights.at[HALF:WEIGHT_ROWS],
        weights.at[WEIGHT_ROWS : WEIGHT_ROWS + HALF],
    )
    sources = (hidden, gain, bias, key_page, value_page, query_w, keyvalue_w, out_w)
    copies = [
        pltpu.make_async_copy(source, target, done.at[at])
        for at, (source, target) in enumerate(zip(sources, targets))
    ]
    for copy in copies:
        copy.start()
    for copy in copies:
        copy.wait()
    values = held[0][...].astype(F32)
    average = jnp.mean(values, axis=-1, keepdims=True)
    centred = values - average
    spread = jnp.mean(centred * centred, axis=-1, keepdims=True)
    normed = (centred * lax.rsqrt(spread + 1e-05) * held[1][...] + held[2][...]).astype(BF16)
    key_rows = held[3][...]
    value_rows = held[4][...]
    for chip in range(CHIPS):
        send[chip, 0:PAGE, :] = key_rows
        send[chip, PAGE:KV_ROWS, :] = value_rows
        for chunk in range(CHUNKS):
            send[chip, KV_ROWS + OWN * chunk : KV_ROWS + OWN * (chunk + 1), :] = normed[
                :, LANES * chunk : LANES * (chunk + 1)
            ]


def project(tokens, weights, queries, keyvalue):
    query_sum = jnp.zeros((LANES, LANES), F32)
    keyvalue_sum = jnp.zeros((CORES * OWN, LANES), F32)
    for chunk in range(CHUNKS):
        first = KV_ROWS + OWN * chunk
        rows = tokens[:, first : first + OWN, :].astype(F32).reshape(LANES, LANES).astype(BF16)
        square = jnp.concatenate([weights[0, chunk, 0:HALF, :], weights[1, chunk, 0:HALF, :]], axis=0)
        query_sum = query_sum + dot_nt(rows, square)
        narrow = jnp.concatenate(
            [
                weights[0, chunk, HALF:WEIGHT_ROWS, :].astype(F32),
                weights[1, chunk, HALF:WEIGHT_ROWS, :].astype(F32),
            ],
            axis=0,
        ).astype(BF16)
        keyvalue_sum = keyvalue_sum + dot_nt(narrow, rows)
    queries[...] = query_sum.astype(BF16)
    rounded = keyvalue_sum.astype(BF16)
    for place in range(CHIPS * CORES):
        keyvalue[place] = rounded


def new_columns(keyvalue, core, first):
    return jnp.concatenate([keyvalue[CORES * chip + core] for chip in range(first, first + CHIPS // 2)], axis=0)


def token_of(index, core):
    return ((index >> 3) << 4) + OWN * core + (index & 7)


def attend(length_ref, core_ref, queries, own, peer, keyvalue, out_w, result):
    length = length_ref[0]
    core = core_ref[0]
    scale = float(LANES) ** (-0.5)
    query_rows = queries[...]
    places = CHIPS * PAGE
    lane = iota((1, places), 1)
    start = lane + PAGE * ((lane * 911) >> 16)
    scored = []
    value_sets = []
    for source, side in ((own, core), (peer, 1 - core)):
        keys = source[:, 0:PAGE, :].astype(F32).reshape(places, LANES).astype(BF16)
        value_sets.append(source[:, PAGE:KV_ROWS, :].astype(F32).reshape(places, LANES).astype(BF16))
        scores = dot_nt(query_rows, keys) * scale
        scored.append(jnp.where(start + PAGE * side < length, scores, NEGATIVE))
    own_token = token_of(iota((LANES, LANES), 0), core)
    for side in range(CORES):
        scores = dot(query_rows, new_columns(keyvalue, side, 0)) * scale
        scored.append(jnp.where(token_of(iota((LANES, LANES), 1), side) <= own_token, scores, NEGATIVE))
    largest = jnp.max(scored[0], axis=1, keepdims=True)
    for scores in scored[1:]:
        largest = jnp.maximum(largest, jnp.max(scores, axis=1, keepdims=True))
    total = jnp.zeros((LANES, 1), F32)
    summed = jnp.zeros((LANES, LANES), F32)
    for which, scores in enumerate(scored):
        terms = jnp.exp(scores - largest)
        total = total + jnp.sum(terms, axis=1, keepdims=True)
        if which < 2:
            summed = summed + dot(terms.astype(BF16), value_sets[which])
        else:
            summed = summed + dot_nt(terms.astype(BF16), new_columns(keyvalue, which - 2, CHIPS // 2))
    attended = (summed / total).astype(BF16)
    for chunk in range(CHUNKS):
        square = jnp.concatenate([out_w[0, chunk], out_w[1, chunk]], axis=0)
        part = dot(attended, square)
        result[:, OWN * chunk : OWN * (chunk + 1), :] = part.reshape(CHIPS, OWN, LANES).astype(BF16)


def add_heads(parts, result):
    total = parts[0].astype(F32)
    for chip in range(1, CHIPS):
        total = total + parts[chip].astype(F32)
    for chunk in range(CHUNKS):
        result[:, LANES * chunk : LANES * (chunk + 1)] = total[OWN * chunk : OWN * (chunk + 1), :].astype(BF16)


def write_pages(length_ref, place_ref, keyvalue, key_page, value_page, new_key, new_value):
    length = length_ref[0]
    base = place_ref[0] * PAGE - length
    offset = iota((PAGE, LANES), 0) + base
    inside = (offset >= 0) & (offset < NEW)
    key_rows = jnp.zeros((PAGE, LANES), F32)
    value_rows = jnp.zeros((PAGE, LANES), F32)
    for side in range(CORES):
        chosen = (offset == token_of(iota((PAGE, LANES), 1), side)).astype(F32).astype(BF16)
        key_rows = key_rows + dot_nt(chosen, new_columns(keyvalue, side, 0))
        value_rows = value_rows + dot_nt(chosen, new_columns(keyvalue, side, CHIPS // 2))
    new_key[...] = jnp.where(inside, key_rows, key_page[...].astype(F32)).astype(BF16)
    new_value[...] = jnp.where(inside, value_rows, value_page[...].astype(F32)).astype(BF16)


def call(kernel, shapes, arguments, scalars=0, held=None):
    space = pltpu.VMEM if held is None else pltpu.HBM
    specs = [
        pl.BlockSpec(memory_space=pltpu.SMEM if at < scalars else space) for at in range(len(arguments))
    ]
    scratch = []
    if held is not None:
        scratch = [pltpu.VMEM(shape, dtype) for shape, dtype in held]
        scratch.append(pltpu.SemaphoreType.DMA((len(arguments),)))
    return pl.pallas_call(
        kernel,
        out_shape=[jax.ShapeDtypeStruct(shape, dtype) for shape, dtype in shapes],
        in_specs=specs,
        out_specs=[pl.BlockSpec(memory_space=pltpu.VMEM)] * len(shapes),
        scratch_shapes=scratch,
        compiler_params=pltpu.CompilerParams(vmem_limit_bytes=48 * 1024 * 1024),
    )(*arguments)


def body(
    hidden_states,
    norm_gain,
    norm_bias,
    query_weight,
    keyvalue_weight,
    out_weight,
    key_cache,
    value_cache,
    cache_length,
):
    place = lax.axis_index("gx").astype(jnp.int32).reshape(1)
    core = place & 1
    send, weights = call(
        prepare,
        [((CHIPS, SEND_ROWS, LANES), BF16), ((WEIGHT_ROWS + HALF, LANES), BF16)],
        (
            hidden_states[0],
            norm_gain.reshape(1, FEATURES),
            norm_bias.reshape(1, FEATURES),
            query_weight.T,
            keyvalue_weight.T,
            out_weight,
            key_cache[0],
            value_cache[0],
        ),
        held=[
            ((OWN, FEATURES), BF16),
            ((1, FEATURES), F32),
            ((1, FEATURES), F32),
            ((PAGE, LANES), BF16),
            ((PAGE, LANES), BF16),
        ],
    )
    own = lax.all_to_all(send, "gx", 0, 0, tiled=True, axis_index_groups=SAME_CORE)
    planes = lax.all_gather(weights, "gy", axis=0, tiled=False)
    own, planes = lax.optimization_barrier((own, planes))
    inner = lax.all_gather(planes[:, :WEIGHT_ROWS], "gx", axis=0, tiled=False, axis_index_groups=ONE_CHIP)
    queries, rows = call(
        project,
        [((LANES, LANES), BF16), ((CHIPS * CORES, CORES * OWN, LANES), BF16)],
        (own, inner),
    )
    keyvalue = lax.all_to_all(rows, "gx", 0, 0, tiled=True)
    peer = lax.ppermute(own[:, :KV_ROWS], "gx", SWAP)
    outer = lax.all_gather(planes[:, WEIGHT_ROWS:], "gx", axis=0, tiled=False, axis_index_groups=ONE_CHIP)
    (parts,) = call(
        attend,
        [((CHIPS, LANES, LANES), BF16)],
        (cache_length, core, queries, own, peer, keyvalue, outer),
        scalars=2,
    )
    collected = lax.all_to_all(parts, "gx", 0, 0, tiled=True, axis_index_groups=SAME_CORE)
    new_key, new_value = call(
        write_pages,
        [((PAGE, LANES), BF16), ((PAGE, LANES), BF16)],
        (cache_length, place, keyvalue, key_cache[0], value_cache[0]),
        scalars=2,
    )
    (out,) = call(add_heads, [((OWN, FEATURES), BF16)], (collected,))
    return (out[None], new_key[None], new_value[None])


def solution(mesh):
    return jax.shard_map(
        body,
        mesh=mesh,
        in_specs=(
            P("gy", "gx", None),
            P(),
            P(),
            P("gy", "gx"),
            P("gy", "gx"),
            P("gx", "gy"),
            P("gy", "gx", None),
            P("gy", "gx", None),
            P("gy"),
        ),
        out_specs=(P("gy", "gx", None), P("gy", "gx", None), P("gy", "gx", None)),
        check_vma=False,
    )
```

```python
import jax
import jax.numpy as jnp
from jax import lax
from jax.experimental import pallas as pl
from jax.experimental.pallas import tpu as pltpu
from jax.sharding import PartitionSpec as P

CHIPS = 16
CORES = 2
LANES = 128
HALF = 64
PAGE = 72
OWN = 8
FEATURES = 2048
CHUNKS = FEATURES // LANES
KV_ROWS = 2 * PAGE
SEND_ROWS = KV_ROWS + OWN * CHUNKS
WEIGHT_ROWS = HALF + OWN
NEW = 256
NEGATIVE = -1e30

SAME_CORE = [[CORES * chip + core for chip in range(CHIPS)] for core in range(CORES)]
ONE_CHIP = [[CORES * chip + core for core in range(CORES)] for chip in range(CHIPS)]
SWAP = [(place, place ^ 1) for place in range(CHIPS * CORES)]

F32 = jnp.float32
BF16 = jnp.bfloat16


def dot(a, b):
    return lax.dot_general(a, b, (((1,), (0,)), ((), ())), preferred_element_type=F32)


def dot_nt(a, b):
    return lax.dot_general(a, b, (((1,), (1,)), ((), ())), preferred_element_type=F32)


def iota(shape, dim):
    return lax.broadcasted_iota(jnp.int32, shape, dim)


def prepare(hidden, gain, bias, query_w, keyvalue_w, out_w, key_page, value_page, send, weights, *scratch):
    held, done = scratch[:-1], scratch[-1]
    targets = held + (
        weights.at[0:HALF],
        weights.at[HALF:WEIGHT_ROWS],
        weights.at[WEIGHT_ROWS : WEIGHT_ROWS + HALF],
    )
    sources = (hidden, gain, bias, key_page, value_page, query_w, keyvalue_w, out_w)
    copies = [
        pltpu.make_async_copy(source, target, done.at[at])
        for at, (source, target) in enumerate(zip(sources, targets))
    ]
    for copy in copies:
        copy.start()
    for copy in copies:
        copy.wait()
    values = held[0][...].astype(F32)
    average = jnp.mean(values, axis=-1, keepdims=True)
    centred = values - average
    spread = jnp.mean(centred * centred, axis=-1, keepdims=True)
    normed = (centred * lax.rsqrt(spread + 1e-05) * held[1][...] + held[2][...]).astype(BF16)
    key_rows = held[3][...]
    value_rows = held[4][...]
    for chip in range(CHIPS):
        send[chip, 0:PAGE, :] = key_rows
        send[chip, PAGE:KV_ROWS, :] = value_rows
        for chunk in range(CHUNKS):
            send[chip, KV_ROWS + OWN * chunk : KV_ROWS + OWN * (chunk + 1), :] = normed[
                :, LANES * chunk : LANES * (chunk + 1)
            ]


def gathered_tokens(tokens):
    pieces = []
    for chunk in range(CHUNKS):
        first = KV_ROWS + OWN * chunk
        pieces.append(tokens[:, first : first + OWN, :].astype(F32).reshape(LANES, LANES).astype(BF16))
    return jnp.concatenate(pieces, axis=1)


def project_keyvalue(tokens, weights, keyvalue):
    narrow = jnp.concatenate(
        [
            jnp.concatenate([weights[core, chunk, HALF:WEIGHT_ROWS, :].astype(F32) for core in range(CORES)], axis=0)
            for chunk in range(CHUNKS)
        ],
        axis=1,
    ).astype(BF16)
    rounded = dot_nt(narrow, gathered_tokens(tokens)).astype(BF16)
    for place in range(CHIPS * CORES):
        keyvalue[place] = rounded


def project_queries(tokens, weights, queries):
    square = jnp.concatenate(
        [
            jnp.concatenate([weights[core, chunk, 0:HALF, :] for core in range(CORES)], axis=0)
            for chunk in range(CHUNKS)
        ],
        axis=1,
    )
    queries[...] = dot_nt(gathered_tokens(tokens), square).astype(BF16)


def new_columns(keyvalue, core, first):
    return jnp.concatenate([keyvalue[CORES * chip + core] for chip in range(first, first + CHIPS // 2)], axis=0)


def token_of(index, core):
    return ((index >> 3) << 4) + OWN * core + (index & 7)


def attend_cached(length_ref, core_ref, queries, own, peer, largest_out, total_out, summed_out):
    length = length_ref[0]
    core = core_ref[0]
    scale = float(LANES) ** (-0.5)
    query_rows = queries[...]
    places = CHIPS * PAGE
    lane = iota((1, places), 1)
    start = lane + PAGE * ((lane * 911) >> 16)
    scored = []
    value_sets = []
    for source, side in ((own, core), (peer, 1 - core)):
        keys = source[:, 0:PAGE, :].astype(F32).reshape(places, LANES).astype(BF16)
        value_sets.append(source[:, PAGE:KV_ROWS, :].astype(F32).reshape(places, LANES).astype(BF16))
        scores = dot_nt(query_rows, keys) * scale
        scored.append(jnp.where(start + PAGE * side < length, scores, NEGATIVE))
    largest = jnp.maximum(
        jnp.max(scored[0], axis=1, keepdims=True), jnp.max(scored[1], axis=1, keepdims=True)
    )
    total = jnp.zeros((LANES, 1), F32)
    summed = jnp.zeros((LANES, LANES), F32)
    for scores, values in zip(scored, value_sets):
        terms = jnp.where(scores > 0.5 * NEGATIVE, jnp.exp(scores - largest), 0.0)
        total = total + jnp.sum(terms, axis=1, keepdims=True)
        summed = summed + dot(terms.astype(BF16), values)
    largest_out[...] = jnp.broadcast_to(largest, (LANES, LANES))
    total_out[...] = jnp.broadcast_to(total, (LANES, LANES))
    summed_out[...] = summed


def attend_new(core_ref, queries, old_largest, old_total, old_summed, keyvalue, planes, peer, result):
    core = core_ref[0]
    scale = float(LANES) ** (-0.5)
    query_rows = queries[...]
    own_token = token_of(iota((LANES, LANES), 0), core)
    scored = []
    for side in range(CORES):
        scores = dot(query_rows, new_columns(keyvalue, side, 0)) * scale
        scored.append(jnp.where(token_of(iota((LANES, LANES), 1), side) <= own_token, scores, NEGATIVE))
    largest = jnp.max(jnp.maximum(scored[0], scored[1]), axis=1, keepdims=True)
    largest = jnp.maximum(old_largest[...], jnp.broadcast_to(largest, (LANES, LANES)))
    factor = jnp.exp(old_largest[...] - largest)
    terms = [jnp.exp(scores - largest) for scores in scored]
    total = old_total[...] * factor + jnp.sum(terms[0] + terms[1], axis=1, keepdims=True)
    summed = old_summed[...] * factor
    for side in range(CORES):
        summed = summed + dot_nt(terms[side].astype(BF16), new_columns(keyvalue, side, CHIPS // 2))
    turned = pltpu.roll(summed, HALF, 1)
    summed = jnp.where(core == 0, summed, turned)
    attended = (summed / total).astype(BF16)
    for chunk in range(CHUNKS):
        square = jnp.concatenate(
            [planes[chunk, WEIGHT_ROWS : WEIGHT_ROWS + HALF, :], peer[chunk, KV_ROWS : KV_ROWS + HALF, :]], axis=0
        )
        part = dot(attended, square)
        result[:, OWN * chunk : OWN * (chunk + 1), :] = part.reshape(CHIPS, OWN, LANES).astype(BF16)


def add_heads(parts, result):
    total = parts[0].astype(F32)
    for chip in range(1, CHIPS):
        total = total + parts[chip].astype(F32)
    for chunk in range(CHUNKS):
        result[:, LANES * chunk : LANES * (chunk + 1)] = total[OWN * chunk : OWN * (chunk + 1), :].astype(BF16)


def write_pages(length_ref, place_ref, keyvalue, key_page, value_page, new_key, new_value):
    length = length_ref[0]
    base = place_ref[0] * PAGE - length
    offset = iota((PAGE, LANES), 0) + base
    inside = (offset >= 0) & (offset < NEW)
    key_rows = jnp.zeros((PAGE, LANES), F32)
    value_rows = jnp.zeros((PAGE, LANES), F32)
    for side in range(CORES):
        chosen = (offset == token_of(iota((PAGE, LANES), 1), side)).astype(F32).astype(BF16)
        key_rows = key_rows + dot_nt(chosen, new_columns(keyvalue, side, 0))
        value_rows = value_rows + dot_nt(chosen, new_columns(keyvalue, side, CHIPS // 2))
    new_key[...] = jnp.where(inside, key_rows, key_page[...].astype(F32)).astype(BF16)
    new_value[...] = jnp.where(inside, value_rows, value_page[...].astype(F32)).astype(BF16)


def call(kernel, shapes, arguments, scalars=0, held=None):
    space = pltpu.VMEM if held is None else pltpu.HBM
    specs = [
        pl.BlockSpec(memory_space=pltpu.SMEM if at < scalars else space) for at in range(len(arguments))
    ]
    scratch = []
    if held is not None:
        scratch = [pltpu.VMEM(shape, dtype) for shape, dtype in held]
        scratch.append(pltpu.SemaphoreType.DMA((len(arguments),)))
    if held is not None:
        arguments = [pltpu.with_memory_space_constraint(argument, pltpu.HBM) for argument in arguments]
    return pl.pallas_call(
        kernel,
        out_shape=[jax.ShapeDtypeStruct(shape, dtype) for shape, dtype in shapes],
        in_specs=specs,
        out_specs=[pl.BlockSpec(memory_space=pltpu.VMEM)] * len(shapes),
        scratch_shapes=scratch,
        compiler_params=pltpu.CompilerParams(vmem_limit_bytes=48 * 1024 * 1024),
    )(*arguments)


def body(
    hidden_states,
    norm_gain,
    norm_bias,
    query_weight,
    keyvalue_weight,
    out_weight,
    key_cache,
    value_cache,
    cache_length,
):
    place = lax.axis_index("gx").astype(jnp.int32).reshape(1)
    core = place & 1
    send, weights = call(
        prepare,
        [((CHIPS, SEND_ROWS, LANES), BF16), ((WEIGHT_ROWS + HALF, LANES), BF16)],
        (
            hidden_states[0],
            norm_gain.reshape(1, FEATURES),
            norm_bias.reshape(1, FEATURES),
            query_weight.T,
            keyvalue_weight.T,
            out_weight,
            key_cache[0],
            value_cache[0],
        ),
        held=[
            ((OWN, FEATURES), BF16),
            ((1, FEATURES), F32),
            ((1, FEATURES), F32),
            ((PAGE, LANES), BF16),
            ((PAGE, LANES), BF16),
        ],
    )
    own = lax.all_to_all(send, "gx", 0, 0, tiled=True, axis_index_groups=SAME_CORE)
    planes = lax.all_gather(weights, "gy", axis=0, tiled=False)
    own, planes = lax.optimization_barrier((own, planes))
    inner = lax.all_gather(planes[:, :WEIGHT_ROWS], "gx", axis=0, tiled=False, axis_index_groups=ONE_CHIP)
    (rows,) = call(
        project_keyvalue,
        [((CHIPS * CORES, CORES * OWN, LANES), BF16)],
        (own, inner),
    )
    keyvalue = lax.all_to_all(rows, "gx", 0, 0, tiled=True)
    swapped = jnp.concatenate([own[:, :KV_ROWS], planes[:, WEIGHT_ROWS:]], axis=1)
    peer = lax.ppermute(swapped, "gx", SWAP)
    (queries,) = call(project_queries, [((LANES, LANES), BF16)], (own, inner))
    largest, total, summed = call(
        attend_cached,
        [((LANES, LANES), F32)] * 3,
        (cache_length, core, queries, own, peer),
        scalars=2,
    )
    (parts,) = call(
        attend_new,
        [((CHIPS, LANES, LANES), BF16)],
        (core, queries, largest, total, summed, keyvalue, planes, peer),
        scalars=1,
    )
    collected = lax.all_to_all(parts, "gx", 0, 0, tiled=True, axis_index_groups=SAME_CORE)
    new_key, new_value = call(
        write_pages,
        [((PAGE, LANES), BF16), ((PAGE, LANES), BF16)],
        (cache_length, place, keyvalue, key_cache[0], value_cache[0]),
        scalars=2,
    )
    (out,) = call(add_heads, [((OWN, FEATURES), BF16)], (collected,))
    return (out[None], new_key[None], new_value[None])


def solution(mesh):
    return jax.shard_map(
        body,
        mesh=mesh,
        in_specs=(
            P("gy", "gx", None),
            P(),
            P(),
            P("gy", "gx"),
            P("gy", "gx"),
            P("gx", "gy"),
            P("gy", "gx", None),
            P("gy", "gx", None),
            P("gy"),
        ),
        out_specs=(P("gy", "gx", None), P("gy", "gx", None), P("gy", "gx", None)),
        check_vma=False,
    )
```

```python
import jax
import jax.numpy as jnp
from jax import lax
from jax.experimental import pallas as pl
from jax.experimental.pallas import tpu as pltpu
from jax.sharding import PartitionSpec as P

CHIPS = 16
CORES = 2
LANES = 128
HALF = 64
PAGE = 72
OWN = 8
FEATURES = 2048
CHUNKS = FEATURES // LANES
KV_ROWS = 2 * PAGE
SEND_ROWS = KV_ROWS + OWN * CHUNKS
WEIGHT_ROWS = HALF + OWN
NEW = 256
NEGATIVE = -1e30

SAME_CORE = [[CORES * chip + core for chip in range(CHIPS)] for core in range(CORES)]
ONE_CHIP = [[CORES * chip + core for core in range(CORES)] for chip in range(CHIPS)]
SWAP = [(place, place ^ 1) for place in range(CHIPS * CORES)]

F32 = jnp.float32
BF16 = jnp.bfloat16


def dot(a, b):
    return lax.dot_general(a, b, (((1,), (0,)), ((), ())), preferred_element_type=F32)


def dot_nt(a, b):
    return lax.dot_general(a, b, (((1,), (1,)), ((), ())), preferred_element_type=F32)


def iota(shape, dim):
    return lax.broadcasted_iota(jnp.int32, shape, dim)


def prepare(hidden, gain, bias, query_w, keyvalue_w, out_w, key_page, value_page, send, weights, *scratch):
    held, done = scratch[:-1], scratch[-1]
    targets = held + (
        weights.at[0:HALF],
        weights.at[HALF:WEIGHT_ROWS],
        weights.at[WEIGHT_ROWS : WEIGHT_ROWS + HALF],
    )
    sources = (hidden, gain, bias, key_page, value_page, query_w, keyvalue_w, out_w)
    copies = [
        pltpu.make_async_copy(source, target, done.at[at])
        for at, (source, target) in enumerate(zip(sources, targets))
    ]
    for copy in copies:
        copy.start()
    for copy in copies:
        copy.wait()
    values = held[0][...].astype(F32)
    average = jnp.mean(values, axis=-1, keepdims=True)
    centred = values - average
    spread = jnp.mean(centred * centred, axis=-1, keepdims=True)
    normed = (centred * lax.rsqrt(spread + 1e-05) * held[1][...] + held[2][...]).astype(BF16)
    key_rows = held[3][...]
    value_rows = held[4][...]
    for chip in range(CHIPS):
        send[chip, 0:PAGE, :] = key_rows
        send[chip, PAGE:KV_ROWS, :] = value_rows
        for chunk in range(CHUNKS):
            send[chip, KV_ROWS + OWN * chunk : KV_ROWS + OWN * (chunk + 1), :] = normed[
                :, LANES * chunk : LANES * (chunk + 1)
            ]


def gathered_tokens(tokens):
    pieces = []
    for chunk in range(CHUNKS):
        first = KV_ROWS + OWN * chunk
        pieces.append(tokens[:, first : first + OWN, :].astype(F32).reshape(LANES, LANES).astype(BF16))
    return jnp.concatenate(pieces, axis=1)


def project_keyvalue(tokens, weights, keyvalue):
    narrow = jnp.concatenate(
        [
            jnp.concatenate([weights[core, chunk, HALF:WEIGHT_ROWS, :].astype(F32) for core in range(CORES)], axis=0)
            for chunk in range(CHUNKS)
        ],
        axis=1,
    ).astype(BF16)
    rounded = dot_nt(narrow, gathered_tokens(tokens)).astype(BF16)
    for chip in range(CHIPS):
        keyvalue[chip] = rounded


def project_queries(tokens, weights):
    square = jnp.concatenate(
        [
            jnp.concatenate([weights[core, chunk, 0:HALF, :] for core in range(CORES)], axis=0)
            for chunk in range(CHUNKS)
        ],
        axis=1,
    )
    return dot_nt(gathered_tokens(tokens), square).astype(BF16)


def new_columns(keyvalue, core, first):
    return jnp.concatenate([keyvalue[core, chip] for chip in range(first, first + CHIPS // 2)], axis=0)


def token_of(index, core):
    return ((index >> 3) << 4) + OWN * core + (index & 7)


def attend_cached(length_ref, own, weights, keys, values, queries, largest_out, total_out, summed_out):
    length = length_ref[0]
    scale = float(LANES) ** (-0.5)
    query_rows = project_queries(own, weights)
    queries[...] = query_rows
    places = CHIPS * PAGE
    lane = iota((1, places), 1)
    start = lane + PAGE * ((lane * 911) >> 16)
    scored = []
    value_sets = []
    for side in range(CORES):
        key_rows = keys[side].astype(F32).reshape(places, LANES).astype(BF16)
        value_sets.append(values[side].astype(F32).reshape(places, LANES).astype(BF16))
        scores = dot_nt(query_rows, key_rows) * scale
        scored.append(jnp.where(start + PAGE * side < length, scores, NEGATIVE))
    largest = jnp.maximum(
        jnp.max(scored[0], axis=1, keepdims=True), jnp.max(scored[1], axis=1, keepdims=True)
    )
    total = jnp.zeros((LANES, 1), F32)
    summed = jnp.zeros((LANES, LANES), F32)
    for scores, value_rows in zip(scored, value_sets):
        terms = jnp.where(scores > 0.5 * NEGATIVE, jnp.exp(scores - largest), 0.0)
        total = total + jnp.sum(terms, axis=1, keepdims=True)
        summed = summed + dot(terms.astype(BF16), value_rows)
    largest_out[...] = jnp.broadcast_to(largest, (LANES, LANES))
    total_out[...] = jnp.broadcast_to(total, (LANES, LANES))
    summed_out[...] = summed


def attend_new(core_ref, queries, old_largest, old_total, old_summed, keyvalue, out_w, result):
    core = core_ref[0]
    scale = float(LANES) ** (-0.5)
    query_rows = queries[...]
    own_token = token_of(iota((LANES, LANES), 0), core)
    scored = []
    for side in range(CORES):
        scores = dot(query_rows, new_columns(keyvalue, side, 0)) * scale
        scored.append(jnp.where(token_of(iota((LANES, LANES), 1), side) <= own_token, scores, NEGATIVE))
    largest = jnp.max(jnp.maximum(scored[0], scored[1]), axis=1, keepdims=True)
    largest = jnp.maximum(old_largest[...], jnp.broadcast_to(largest, (LANES, LANES)))
    factor = jnp.exp(old_largest[...] - largest)
    terms = [jnp.exp(scores - largest) for scores in scored]
    total = old_total[...] * factor + jnp.sum(terms[0] + terms[1], axis=1, keepdims=True)
    summed = old_summed[...] * factor
    for side in range(CORES):
        summed = summed + dot_nt(terms[side].astype(BF16), new_columns(keyvalue, side, CHIPS // 2))
    attended = (summed / total).astype(BF16)
    for chunk in range(CHUNKS):
        square = jnp.concatenate([out_w[0, chunk], out_w[1, chunk]], axis=0)
        part = dot(attended, square)
        result[:, OWN * chunk : OWN * (chunk + 1), :] = part.reshape(CHIPS, OWN, LANES).astype(BF16)


def add_heads(parts, result):
    total = parts[0].astype(F32)
    for chip in range(1, CHIPS):
        total = total + parts[chip].astype(F32)
    for chunk in range(CHUNKS):
        result[:, LANES * chunk : LANES * (chunk + 1)] = total[OWN * chunk : OWN * (chunk + 1), :].astype(BF16)


def write_pages(length_ref, place_ref, keyvalue, key_page, value_page, new_key, new_value):
    length = length_ref[0]
    base = place_ref[0] * PAGE - length
    offset = iota((PAGE, LANES), 0) + base
    inside = (offset >= 0) & (offset < NEW)
    key_rows = jnp.zeros((PAGE, LANES), F32)
    value_rows = jnp.zeros((PAGE, LANES), F32)
    for side in range(CORES):
        chosen = (offset == token_of(iota((PAGE, LANES), 1), side)).astype(F32).astype(BF16)
        key_rows = key_rows + dot_nt(chosen, new_columns(keyvalue, side, 0))
        value_rows = value_rows + dot_nt(chosen, new_columns(keyvalue, side, CHIPS // 2))
    new_key[...] = jnp.where(inside, key_rows, key_page[...].astype(F32)).astype(BF16)
    new_value[...] = jnp.where(inside, value_rows, value_page[...].astype(F32)).astype(BF16)


def call(kernel, shapes, arguments, scalars=0, held=None):
    space = pltpu.VMEM if held is None else pltpu.HBM
    specs = [
        pl.BlockSpec(memory_space=pltpu.SMEM if at < scalars else space) for at in range(len(arguments))
    ]
    scratch = []
    if held is not None:
        scratch = [pltpu.VMEM(shape, dtype) for shape, dtype in held]
        scratch.append(pltpu.SemaphoreType.DMA((len(arguments),)))
    if held is not None:
        arguments = [pltpu.with_memory_space_constraint(argument, pltpu.HBM) for argument in arguments]
    return pl.pallas_call(
        kernel,
        out_shape=[jax.ShapeDtypeStruct(shape, dtype) for shape, dtype in shapes],
        in_specs=specs,
        out_specs=[pl.BlockSpec(memory_space=pltpu.VMEM)] * len(shapes),
        scratch_shapes=scratch,
        compiler_params=pltpu.CompilerParams(vmem_limit_bytes=48 * 1024 * 1024),
    )(*arguments)


def body(
    hidden_states,
    norm_gain,
    norm_bias,
    query_weight,
    keyvalue_weight,
    out_weight,
    key_cache,
    value_cache,
    cache_length,
):
    place = lax.axis_index("gx").astype(jnp.int32).reshape(1)
    core = place & 1
    send, weights = call(
        prepare,
        [((CHIPS, SEND_ROWS, LANES), BF16), ((WEIGHT_ROWS + HALF, LANES), BF16)],
        (
            hidden_states[0],
            norm_gain.reshape(1, FEATURES),
            norm_bias.reshape(1, FEATURES),
            query_weight.T,
            keyvalue_weight.T,
            out_weight,
            key_cache[0],
            value_cache[0],
        ),
        held=[
            ((OWN, FEATURES), BF16),
            ((1, FEATURES), F32),
            ((1, FEATURES), F32),
            ((PAGE, LANES), BF16),
            ((PAGE, LANES), BF16),
        ],
    )
    own = lax.all_to_all(send, "gx", 0, 0, tiled=True, axis_index_groups=SAME_CORE)
    planes = lax.all_gather(weights, "gy", axis=0, tiled=False)
    own, planes = lax.optimization_barrier((own, planes))
    inner = lax.all_gather(planes[:, :WEIGHT_ROWS], "gx", axis=0, tiled=False, axis_index_groups=ONE_CHIP)
    (rows,) = call(project_keyvalue, [((CHIPS, CORES * OWN, LANES), BF16)], (own, inner))
    own, inner, planes, rows = lax.optimization_barrier((own, inner, planes, rows))
    columns = lax.all_to_all(rows, "gx", 0, 0, tiled=True, axis_index_groups=SAME_CORE)
    outer = lax.all_gather(planes[:, WEIGHT_ROWS:], "gx", axis=0, tiled=False, axis_index_groups=ONE_CHIP)
    keys = lax.all_gather(own[:, :PAGE], "gx", axis=0, tiled=False, axis_index_groups=ONE_CHIP)
    values = lax.all_gather(own[:, PAGE:KV_ROWS], "gx", axis=0, tiled=False, axis_index_groups=ONE_CHIP)
    queries, largest, total, summed = call(
        attend_cached,
        [((LANES, LANES), BF16)] + [((LANES, LANES), F32)] * 3,
        (cache_length, own, inner, keys, values),
        scalars=1,
    )
    columns, outer, summed = lax.optimization_barrier((columns, outer, summed))
    keyvalue = lax.all_gather(columns, "gx", axis=0, tiled=False, axis_index_groups=ONE_CHIP)
    (parts,) = call(
        attend_new,
        [((CHIPS, LANES, LANES), BF16)],
        (core, queries, largest, total, summed, keyvalue, outer),
        scalars=1,
    )
    collected = lax.all_to_all(parts, "gx", 0, 0, tiled=True, axis_index_groups=SAME_CORE)
    new_key, new_value = call(
        write_pages,
        [((PAGE, LANES), BF16), ((PAGE, LANES), BF16)],
        (cache_length, place, keyvalue, key_cache[0], value_cache[0]),
        scalars=2,
    )
    (out,) = call(add_heads, [((OWN, FEATURES), BF16)], (collected,))
    return (out[None], new_key[None], new_value[None])


def solution(mesh):
    return jax.shard_map(
        body,
        mesh=mesh,
        in_specs=(
            P("gy", "gx", None),
            P(),
            P(),
            P("gy", "gx"),
            P("gy", "gx"),
            P("gx", "gy"),
            P("gy", "gx", None),
            P("gy", "gx", None),
            P("gy"),
        ),
        out_specs=(P("gy", "gx", None), P("gy", "gx", None), P("gy", "gx", None)),
        check_vma=False,
    )
```

```python
import jax
import jax.numpy as jnp
from jax import lax
from jax.experimental import pallas as pl
from jax.experimental.pallas import tpu as pltpu
from jax.sharding import PartitionSpec as P

CHIPS = 16
CORES = 2
LANES = 128
HALF = 64
PAGE = 72
OWN = 8
FEATURES = 2048
CHUNKS = FEATURES // LANES
KV_ROWS = 2 * PAGE
SEND_ROWS = KV_ROWS + OWN * CHUNKS
WEIGHT_ROWS = HALF + OWN
NEW = 256
NEGATIVE = -1e30

SAME_CORE = [[CORES * chip + core for chip in range(CHIPS)] for core in range(CORES)]
ONE_CHIP = [[CORES * chip + core for core in range(CORES)] for chip in range(CHIPS)]
SWAP = [(place, place ^ 1) for place in range(CHIPS * CORES)]

F32 = jnp.float32
BF16 = jnp.bfloat16


def dot(a, b):
    return lax.dot_general(a, b, (((1,), (0,)), ((), ())), preferred_element_type=F32)


def dot_nt(a, b):
    return lax.dot_general(a, b, (((1,), (1,)), ((), ())), preferred_element_type=F32)


def iota(shape, dim):
    return lax.broadcasted_iota(jnp.int32, shape, dim)


def prepare(hidden, gain, bias, query_w, keyvalue_w, out_w, key_page, value_page, send, weights, *scratch):
    held, done = scratch[:-1], scratch[-1]
    targets = held + (
        weights.at[0:HALF],
        weights.at[HALF:WEIGHT_ROWS],
        weights.at[WEIGHT_ROWS : WEIGHT_ROWS + HALF],
    )
    sources = (hidden, gain, bias, key_page, value_page, query_w, keyvalue_w, out_w)
    copies = [
        pltpu.make_async_copy(source, target, done.at[at])
        for at, (source, target) in enumerate(zip(sources, targets))
    ]
    for copy in copies:
        copy.start()
    for copy in copies:
        copy.wait()
    values = held[0][...].astype(F32)
    average = jnp.mean(values, axis=-1, keepdims=True)
    centred = values - average
    spread = jnp.mean(centred * centred, axis=-1, keepdims=True)
    normed = (centred * lax.rsqrt(spread + 1e-05) * held[1][...] + held[2][...]).astype(BF16)
    key_rows = held[3][...]
    value_rows = held[4][...]
    for chip in range(CHIPS):
        send[chip, 0:PAGE, :] = key_rows
        send[chip, PAGE:KV_ROWS, :] = value_rows
        for chunk in range(CHUNKS):
            send[chip, KV_ROWS + OWN * chunk : KV_ROWS + OWN * (chunk + 1), :] = normed[
                :, LANES * chunk : LANES * (chunk + 1)
            ]


def gathered_tokens(tokens):
    pieces = []
    for chunk in range(CHUNKS):
        first = KV_ROWS + OWN * chunk
        pieces.append(tokens[:, first : first + OWN, :].astype(F32).reshape(LANES, LANES).astype(BF16))
    return jnp.concatenate(pieces, axis=1)


def project_keyvalue(tokens, weights, keyvalue):
    narrow = jnp.concatenate(
        [
            jnp.concatenate([weights[core, chunk, HALF:WEIGHT_ROWS, :].astype(F32) for core in range(CORES)], axis=0)
            for chunk in range(CHUNKS)
        ],
        axis=1,
    ).astype(BF16)
    rounded = dot_nt(narrow, gathered_tokens(tokens)).astype(BF16)
    for chip in range(CHIPS):
        keyvalue[chip] = rounded


def project_queries(tokens, weights):
    square = jnp.concatenate(
        [
            jnp.concatenate([weights[core, chunk, 0:HALF, :] for core in range(CORES)], axis=0)
            for chunk in range(CHUNKS)
        ],
        axis=1,
    )
    return dot_nt(gathered_tokens(tokens), square).astype(BF16)


def new_columns(keyvalue, core, first):
    return jnp.concatenate([keyvalue[core, chip] for chip in range(first, first + CHIPS // 2)], axis=0)


def token_of(index, core):
    return ((index >> 3) << 4) + OWN * core + (index & 7)


def attend_cached(length_ref, core_ref, own, weights, peer, queries, largest_out, total_out, summed_out):
    length = length_ref[0]
    core = core_ref[0]
    scale = float(LANES) ** (-0.5)
    query_rows = project_queries(own, weights)
    queries[...] = query_rows
    places = CHIPS * PAGE
    lane = iota((1, places), 1)
    start = lane + PAGE * ((lane * 911) >> 16)
    scored = []
    value_sets = []
    for source, side in ((own, core), (peer, 1 - core)):
        keys = source[:, 0:PAGE, :].astype(F32).reshape(places, LANES).astype(BF16)
        value_sets.append(source[:, PAGE:KV_ROWS, :].astype(F32).reshape(places, LANES).astype(BF16))
        scores = dot_nt(query_rows, keys) * scale
        scored.append(jnp.where(start + PAGE * side < length, scores, NEGATIVE))
    largest = jnp.maximum(
        jnp.max(scored[0], axis=1, keepdims=True), jnp.max(scored[1], axis=1, keepdims=True)
    )
    total = jnp.zeros((LANES, 1), F32)
    summed = jnp.zeros((LANES, LANES), F32)
    for scores, values in zip(scored, value_sets):
        terms = jnp.where(scores > 0.5 * NEGATIVE, jnp.exp(scores - largest), 0.0)
        total = total + jnp.sum(terms, axis=1, keepdims=True)
        summed = summed + dot(terms.astype(BF16), values)
    largest_out[...] = jnp.broadcast_to(largest, (LANES, LANES))
    total_out[...] = jnp.broadcast_to(total, (LANES, LANES))
    summed_out[...] = summed


def attend_new(core_ref, queries, old_largest, old_total, old_summed, keyvalue, out_w, result):
    core = core_ref[0]
    scale = float(LANES) ** (-0.5)
    query_rows = queries[...]
    own_token = token_of(iota((LANES, LANES), 0), core)
    scored = []
    for side in range(CORES):
        scores = dot(query_rows, new_columns(keyvalue, side, 0)) * scale
        scored.append(jnp.where(token_of(iota((LANES, LANES), 1), side) <= own_token, scores, NEGATIVE))
    largest = jnp.max(jnp.maximum(scored[0], scored[1]), axis=1, keepdims=True)
    largest = jnp.maximum(old_largest[...], jnp.broadcast_to(largest, (LANES, LANES)))
    factor = jnp.exp(old_largest[...] - largest)
    terms = [jnp.exp(scores - largest) for scores in scored]
    total = old_total[...] * factor + jnp.sum(terms[0] + terms[1], axis=1, keepdims=True)
    summed = old_summed[...] * factor
    for side in range(CORES):
        summed = summed + dot_nt(terms[side].astype(BF16), new_columns(keyvalue, side, CHIPS // 2))
    attended = (summed / total).astype(BF16)
    for chunk in range(CHUNKS):
        square = jnp.concatenate([out_w[0, chunk], out_w[1, chunk]], axis=0)
        part = dot(attended, square)
        result[:, OWN * chunk : OWN * (chunk + 1), :] = part.reshape(CHIPS, OWN, LANES).astype(BF16)


def add_heads(parts, result):
    total = parts[0].astype(F32)
    for chip in range(1, CHIPS):
        total = total + parts[chip].astype(F32)
    for chunk in range(CHUNKS):
        result[:, LANES * chunk : LANES * (chunk + 1)] = total[OWN * chunk : OWN * (chunk + 1), :].astype(BF16)


def write_pages(length_ref, place_ref, keyvalue, key_page, value_page, new_key, new_value):
    length = length_ref[0]
    base = place_ref[0] * PAGE - length
    offset = iota((PAGE, LANES), 0) + base
    inside = (offset >= 0) & (offset < NEW)
    key_rows = jnp.zeros((PAGE, LANES), F32)
    value_rows = jnp.zeros((PAGE, LANES), F32)
    for side in range(CORES):
        chosen = (offset == token_of(iota((PAGE, LANES), 1), side)).astype(F32).astype(BF16)
        key_rows = key_rows + dot_nt(chosen, new_columns(keyvalue, side, 0))
        value_rows = value_rows + dot_nt(chosen, new_columns(keyvalue, side, CHIPS // 2))
    new_key[...] = jnp.where(inside, key_rows, key_page[...].astype(F32)).astype(BF16)
    new_value[...] = jnp.where(inside, value_rows, value_page[...].astype(F32)).astype(BF16)


def call(kernel, shapes, arguments, scalars=0, held=None):
    space = pltpu.VMEM if held is None else pltpu.HBM
    specs = [
        pl.BlockSpec(memory_space=pltpu.SMEM if at < scalars else space) for at in range(len(arguments))
    ]
    scratch = []
    if held is not None:
        scratch = [pltpu.VMEM(shape, dtype) for shape, dtype in held]
        scratch.append(pltpu.SemaphoreType.DMA((len(arguments),)))
    if held is not None:
        arguments = [pltpu.with_memory_space_constraint(argument, pltpu.HBM) for argument in arguments]
    return pl.pallas_call(
        kernel,
        out_shape=[jax.ShapeDtypeStruct(shape, dtype) for shape, dtype in shapes],
        in_specs=specs,
        out_specs=[pl.BlockSpec(memory_space=pltpu.VMEM)] * len(shapes),
        scratch_shapes=scratch,
        compiler_params=pltpu.CompilerParams(vmem_limit_bytes=48 * 1024 * 1024),
    )(*arguments)


def body(
    hidden_states,
    norm_gain,
    norm_bias,
    query_weight,
    keyvalue_weight,
    out_weight,
    key_cache,
    value_cache,
    cache_length,
):
    place = lax.axis_index("gx").astype(jnp.int32).reshape(1)
    core = place & 1
    send, weights = call(
        prepare,
        [((CHIPS, SEND_ROWS, LANES), BF16), ((WEIGHT_ROWS + HALF, LANES), BF16)],
        (
            hidden_states[0],
            norm_gain.reshape(1, FEATURES),
            norm_bias.reshape(1, FEATURES),
            query_weight.T,
            keyvalue_weight.T,
            out_weight,
            key_cache[0],
            value_cache[0],
        ),
        held=[
            ((OWN, FEATURES), BF16),
            ((1, FEATURES), F32),
            ((1, FEATURES), F32),
            ((PAGE, LANES), BF16),
            ((PAGE, LANES), BF16),
        ],
    )
    own = lax.all_to_all(send, "gx", 0, 0, tiled=True, axis_index_groups=SAME_CORE)
    planes = lax.all_gather(weights, "gy", axis=0, tiled=False)
    own, planes = lax.optimization_barrier((own, planes))
    inner = lax.all_gather(planes[:, :WEIGHT_ROWS], "gx", axis=0, tiled=False, axis_index_groups=ONE_CHIP)
    (rows,) = call(project_keyvalue, [((CHIPS, CORES * OWN, LANES), BF16)], (own, inner))
    own, inner, planes, rows = lax.optimization_barrier((own, inner, planes, rows))
    columns = lax.all_to_all(rows, "gx", 0, 0, tiled=True, axis_index_groups=SAME_CORE)
    outer = lax.all_gather(planes[:, WEIGHT_ROWS:], "gx", axis=0, tiled=False, axis_index_groups=ONE_CHIP)
    peer = lax.ppermute(own[:, :KV_ROWS], "gx", SWAP)
    queries, largest, total, summed = call(
        attend_cached,
        [((LANES, LANES), BF16)] + [((LANES, LANES), F32)] * 3,
        (cache_length, core, own, inner, peer),
        scalars=2,
    )
    columns, outer, summed = lax.optimization_barrier((columns, outer, summed))
    keyvalue = lax.all_gather(columns, "gx", axis=0, tiled=False, axis_index_groups=ONE_CHIP)
    (parts,) = call(
        attend_new,
        [((CHIPS, LANES, LANES), BF16)],
        (core, queries, largest, total, summed, keyvalue, outer),
        scalars=1,
    )
    collected = lax.all_to_all(parts, "gx", 0, 0, tiled=True, axis_index_groups=SAME_CORE)
    new_key, new_value = call(
        write_pages,
        [((PAGE, LANES), BF16), ((PAGE, LANES), BF16)],
        (cache_length, place, keyvalue, key_cache[0], value_cache[0]),
        scalars=2,
    )
    (out,) = call(add_heads, [((OWN, FEATURES), BF16)], (collected,))
    return (out[None], new_key[None], new_value[None])


def solution(mesh):
    return jax.shard_map(
        body,
        mesh=mesh,
        in_specs=(
            P("gy", "gx", None),
            P(),
            P(),
            P("gy", "gx"),
            P("gy", "gx"),
            P("gx", "gy"),
            P("gy", "gx", None),
            P("gy", "gx", None),
            P("gy"),
        ),
        out_specs=(P("gy", "gx", None), P("gy", "gx", None), P("gy", "gx", None)),
        check_vma=False,
    )
```

```python
import jax
import jax.numpy as jnp
from jax import lax
from jax.experimental import pallas as pl
from jax.experimental.pallas import tpu as pltpu
from jax.sharding import PartitionSpec as P

CHIPS = 16
CORES = 2
LANES = 128
HALF = 64
PAGE = 72
OWN = 8
FEATURES = 2048
CHUNKS = FEATURES // LANES
KV_ROWS = 2 * PAGE
SEND_ROWS = KV_ROWS + OWN * CHUNKS
WEIGHT_ROWS = HALF + OWN
NEW = 256
NEGATIVE = -1e30

FIRST = 10
SAME_CORE = [[CORES * ((at + FIRST) % CHIPS) + core for at in range(CHIPS)] for core in range(CORES)]
ONE_CHIP = [[CORES * chip + core for core in range(CORES)] for chip in range(CHIPS)]
SWAP = [(place, place ^ 1) for place in range(CHIPS * CORES)]

F32 = jnp.float32
BF16 = jnp.bfloat16


def dot(a, b):
    return lax.dot_general(a, b, (((1,), (0,)), ((), ())), preferred_element_type=F32)


def dot_nt(a, b):
    return lax.dot_general(a, b, (((1,), (1,)), ((), ())), preferred_element_type=F32)


def iota(shape, dim):
    return lax.broadcasted_iota(jnp.int32, shape, dim)


def prepare(hidden, gain, bias, query_w, keyvalue_w, out_w, key_page, value_page, send, weights, *scratch):
    held, done = scratch[:-1], scratch[-1]
    targets = held + (
        weights.at[0:HALF],
        weights.at[HALF:WEIGHT_ROWS],
        weights.at[WEIGHT_ROWS : WEIGHT_ROWS + HALF],
    )
    sources = (hidden, gain, bias, key_page, value_page, query_w, keyvalue_w, out_w)
    copies = [
        pltpu.make_async_copy(source, target, done.at[at])
        for at, (source, target) in enumerate(zip(sources, targets))
    ]
    for copy in copies:
        copy.start()
    for copy in copies:
        copy.wait()
    values = held[0][...].astype(F32)
    average = jnp.mean(values, axis=-1, keepdims=True)
    centred = values - average
    spread = jnp.mean(centred * centred, axis=-1, keepdims=True)
    normed = (centred * lax.rsqrt(spread + 1e-05) * held[1][...] + held[2][...]).astype(BF16)
    key_rows = held[3][...]
    value_rows = held[4][...]
    for chip in range(CHIPS):
        send[chip, 0:PAGE, :] = key_rows
        send[chip, PAGE:KV_ROWS, :] = value_rows
        for chunk in range(CHUNKS):
            send[chip, KV_ROWS + OWN * chunk : KV_ROWS + OWN * (chunk + 1), :] = normed[
                :, LANES * chunk : LANES * (chunk + 1)
            ]


def gathered_tokens(tokens):
    pieces = []
    for chunk in range(CHUNKS):
        first = KV_ROWS + OWN * chunk
        pieces.append(tokens[:, first : first + OWN, :].astype(F32).reshape(LANES, LANES).astype(BF16))
    return jnp.concatenate(pieces, axis=1)


def project_keyvalue(tokens, weights, keyvalue):
    narrow = jnp.concatenate(
        [
            jnp.concatenate([weights[core, chunk, HALF:WEIGHT_ROWS, :].astype(F32) for core in range(CORES)], axis=0)
            for chunk in range(CHUNKS)
        ],
        axis=1,
    ).astype(BF16)
    rounded = dot_nt(narrow, gathered_tokens(tokens)).astype(BF16)
    for place in range(CHIPS * CORES):
        keyvalue[place] = rounded


def project_queries(tokens, weights, queries):
    square = jnp.concatenate(
        [
            jnp.concatenate([weights[core, chunk, 0:HALF, :] for core in range(CORES)], axis=0)
            for chunk in range(CHUNKS)
        ],
        axis=1,
    )
    queries[...] = dot_nt(gathered_tokens(tokens), square).astype(BF16)


def new_columns(keyvalue, core, first):
    return jnp.concatenate([keyvalue[CORES * chip + core] for chip in range(first, first + CHIPS // 2)], axis=0)


def token_of(index, core):
    chip = ((index >> 3) + FIRST) & (CHIPS - 1)
    return (chip << 4) + OWN * core + (index & 7)


def attend_cached(length_ref, core_ref, queries, own, peer, largest_out, total_out, summed_out):
    length = length_ref[0]
    core = core_ref[0]
    scale = float(LANES) ** (-0.5)
    query_rows = queries[...]
    places = CHIPS * PAGE
    lane = iota((1, places), 1)
    at = (lane * 911) >> 16
    chip = (at + FIRST) & (CHIPS - 1)
    start = lane - PAGE * at + KV_ROWS * chip
    scored = []
    value_sets = []
    for source, side in ((own, core), (peer, 1 - core)):
        keys = source[:, 0:PAGE, :].astype(F32).reshape(places, LANES).astype(BF16)
        value_sets.append(source[:, PAGE:KV_ROWS, :].astype(F32).reshape(places, LANES).astype(BF16))
        scores = dot_nt(query_rows, keys) * scale
        scored.append(jnp.where(start + PAGE * side < length, scores, NEGATIVE))
    largest = jnp.maximum(
        jnp.max(scored[0], axis=1, keepdims=True), jnp.max(scored[1], axis=1, keepdims=True)
    )
    total = jnp.zeros((LANES, 1), F32)
    summed = jnp.zeros((LANES, LANES), F32)
    for scores, values in zip(scored, value_sets):
        terms = jnp.where(scores > 0.5 * NEGATIVE, jnp.exp(scores - largest), 0.0)
        total = total + jnp.sum(terms, axis=1, keepdims=True)
        summed = summed + dot(terms.astype(BF16), values)
    largest_out[...] = jnp.broadcast_to(largest, (LANES, LANES))
    total_out[...] = jnp.broadcast_to(total, (LANES, LANES))
    summed_out[...] = summed


def attend_new(core_ref, queries, old_largest, old_total, old_summed, keyvalue, planes, peer, result):
    core = core_ref[0]
    scale = float(LANES) ** (-0.5)
    query_rows = queries[...]
    own_token = token_of(iota((LANES, LANES), 0), core)
    scored = []
    for side in range(CORES):
        scores = dot(query_rows, new_columns(keyvalue, side, 0)) * scale
        scored.append(jnp.where(token_of(iota((LANES, LANES), 1), side) <= own_token, scores, NEGATIVE))
    largest = jnp.max(jnp.maximum(scored[0], scored[1]), axis=1, keepdims=True)
    largest = jnp.maximum(old_largest[...], jnp.broadcast_to(largest, (LANES, LANES)))
    factor = jnp.exp(old_largest[...] - largest)
    terms = [jnp.exp(scores - largest) for scores in scored]
    total = old_total[...] * factor + jnp.sum(terms[0] + terms[1], axis=1, keepdims=True)
    summed = old_summed[...] * factor
    for side in range(CORES):
        summed = summed + dot_nt(terms[side].astype(BF16), new_columns(keyvalue, side, CHIPS // 2))
    turned = pltpu.roll(summed, HALF, 1)
    summed = jnp.where(core == 0, summed, turned)
    attended = (summed / total).astype(BF16)
    for chunk in range(CHUNKS):
        square = jnp.concatenate(
            [planes[chunk, WEIGHT_ROWS : WEIGHT_ROWS + HALF, :], peer[chunk, KV_ROWS : KV_ROWS + HALF, :]], axis=0
        )
        part = dot(attended, square)
        result[:, OWN * chunk : OWN * (chunk + 1), :] = part.reshape(CHIPS, OWN, LANES).astype(BF16)


def add_heads(parts, result):
    total = parts[0].astype(F32)
    for chip in range(1, CHIPS):
        total = total + parts[chip].astype(F32)
    for chunk in range(CHUNKS):
        result[:, LANES * chunk : LANES * (chunk + 1)] = total[OWN * chunk : OWN * (chunk + 1), :].astype(BF16)


def write_pages(length_ref, place_ref, keyvalue, key_page, value_page, new_key, new_value):
    length = length_ref[0]
    base = place_ref[0] * PAGE - length
    offset = iota((PAGE, LANES), 0) + base
    inside = (offset >= 0) & (offset < NEW)
    key_rows = jnp.zeros((PAGE, LANES), F32)
    value_rows = jnp.zeros((PAGE, LANES), F32)
    for side in range(CORES):
        chosen = (offset == token_of(iota((PAGE, LANES), 1), side)).astype(F32).astype(BF16)
        key_rows = key_rows + dot_nt(chosen, new_columns(keyvalue, side, 0))
        value_rows = value_rows + dot_nt(chosen, new_columns(keyvalue, side, CHIPS // 2))
    new_key[...] = jnp.where(inside, key_rows, key_page[...].astype(F32)).astype(BF16)
    new_value[...] = jnp.where(inside, value_rows, value_page[...].astype(F32)).astype(BF16)


def call(kernel, shapes, arguments, scalars=0, held=None):
    space = pltpu.VMEM if held is None else pltpu.HBM
    specs = [
        pl.BlockSpec(memory_space=pltpu.SMEM if at < scalars else space) for at in range(len(arguments))
    ]
    scratch = []
    if held is not None:
        scratch = [pltpu.VMEM(shape, dtype) for shape, dtype in held]
        scratch.append(pltpu.SemaphoreType.DMA((len(arguments),)))
    if held is not None:
        arguments = [pltpu.with_memory_space_constraint(argument, pltpu.HBM) for argument in arguments]
    return pl.pallas_call(
        kernel,
        out_shape=[jax.ShapeDtypeStruct(shape, dtype) for shape, dtype in shapes],
        in_specs=specs,
        out_specs=[pl.BlockSpec(memory_space=pltpu.VMEM)] * len(shapes),
        scratch_shapes=scratch,
        compiler_params=pltpu.CompilerParams(vmem_limit_bytes=48 * 1024 * 1024),
    )(*arguments)


def body(
    hidden_states,
    norm_gain,
    norm_bias,
    query_weight,
    keyvalue_weight,
    out_weight,
    key_cache,
    value_cache,
    cache_length,
):
    place = lax.axis_index("gx").astype(jnp.int32).reshape(1)
    core = place & 1
    send, weights = call(
        prepare,
        [((CHIPS, SEND_ROWS, LANES), BF16), ((WEIGHT_ROWS + HALF, LANES), BF16)],
        (
            hidden_states[0],
            norm_gain.reshape(1, FEATURES),
            norm_bias.reshape(1, FEATURES),
            query_weight.T,
            keyvalue_weight.T,
            out_weight,
            key_cache[0],
            value_cache[0],
        ),
        held=[
            ((OWN, FEATURES), BF16),
            ((1, FEATURES), F32),
            ((1, FEATURES), F32),
            ((PAGE, LANES), BF16),
            ((PAGE, LANES), BF16),
        ],
    )
    own = lax.all_to_all(send, "gx", 0, 0, tiled=True, axis_index_groups=SAME_CORE)
    planes = lax.all_gather(weights, "gy", axis=0, tiled=False)
    own, planes = lax.optimization_barrier((own, planes))
    inner = lax.all_gather(planes[:, :WEIGHT_ROWS], "gx", axis=0, tiled=False, axis_index_groups=ONE_CHIP)
    (rows,) = call(
        project_keyvalue,
        [((CHIPS * CORES, CORES * OWN, LANES), BF16)],
        (own, inner),
    )
    keyvalue = lax.all_to_all(rows, "gx", 0, 0, tiled=True)
    swapped = jnp.concatenate([own[:, :KV_ROWS], planes[:, WEIGHT_ROWS:]], axis=1)
    peer = lax.ppermute(swapped, "gx", SWAP)
    (queries,) = call(project_queries, [((LANES, LANES), BF16)], (own, inner))
    largest, total, summed = call(
        attend_cached,
        [((LANES, LANES), F32)] * 3,
        (cache_length, core, queries, own, peer),
        scalars=2,
    )
    (parts,) = call(
        attend_new,
        [((CHIPS, LANES, LANES), BF16)],
        (core, queries, largest, total, summed, keyvalue, planes, peer),
        scalars=1,
    )
    collected = lax.all_to_all(parts, "gx", 0, 0, tiled=True, axis_index_groups=SAME_CORE)
    new_key, new_value = call(
        write_pages,
        [((PAGE, LANES), BF16), ((PAGE, LANES), BF16)],
        (cache_length, place, keyvalue, key_cache[0], value_cache[0]),
        scalars=2,
    )
    (out,) = call(add_heads, [((OWN, FEATURES), BF16)], (collected,))
    return (out[None], new_key[None], new_value[None])


def solution(mesh):
    return jax.shard_map(
        body,
        mesh=mesh,
        in_specs=(
            P("gy", "gx", None),
            P(),
            P(),
            P("gy", "gx"),
            P("gy", "gx"),
            P("gx", "gy"),
            P("gy", "gx", None),
            P("gy", "gx", None),
            P("gy"),
        ),
        out_specs=(P("gy", "gx", None), P("gy", "gx", None), P("gy", "gx", None)),
        check_vma=False,
    )
```

```python
import jax
import jax.numpy as jnp
from jax import lax
from jax.experimental import pallas as pl
from jax.experimental.pallas import tpu as pltpu
from jax.sharding import PartitionSpec as P

CHIPS = 16
CORES = 2
LANES = 128
HALF = 64
PAGE = 72
OWN = 8
FEATURES = 2048
CHUNKS = FEATURES // LANES
KV_ROWS = 2 * PAGE
SEND_ROWS = KV_ROWS + OWN * CHUNKS
WEIGHT_ROWS = HALF + OWN
NEW = 256
NEGATIVE = -1e30

FIRST = 10
SAME_CORE = [[CORES * ((at + FIRST) % CHIPS) + core for at in range(CHIPS)] for core in range(CORES)]
ONE_CHIP = [[CORES * chip + core for core in range(CORES)] for chip in range(CHIPS)]
SWAP = [(place, place ^ 1) for place in range(CHIPS * CORES)]

F32 = jnp.float32
BF16 = jnp.bfloat16


def dot(a, b):
    return lax.dot_general(a, b, (((1,), (0,)), ((), ())), preferred_element_type=F32)


def dot_nt(a, b):
    return lax.dot_general(a, b, (((1,), (1,)), ((), ())), preferred_element_type=F32)


def iota(shape, dim):
    return lax.broadcasted_iota(jnp.int32, shape, dim)


def prepare(hidden, gain, bias, query_w, keyvalue_w, out_w, key_page, value_page, send, weights, *scratch):
    held, done = scratch[:-1], scratch[-1]
    targets = held + (
        weights.at[0:HALF],
        weights.at[HALF:WEIGHT_ROWS],
        weights.at[WEIGHT_ROWS : WEIGHT_ROWS + HALF],
    )
    sources = (hidden, gain, bias, key_page, value_page, query_w, keyvalue_w, out_w)
    copies = [
        pltpu.make_async_copy(source, target, done.at[at])
        for at, (source, target) in enumerate(zip(sources, targets))
    ]
    for copy in copies:
        copy.start()
    for copy in copies:
        copy.wait()
    values = held[0][...].astype(F32)
    average = jnp.mean(values, axis=-1, keepdims=True)
    centred = values - average
    spread = jnp.mean(centred * centred, axis=-1, keepdims=True)
    normed = (centred * lax.rsqrt(spread + 1e-05) * held[1][...] + held[2][...]).astype(BF16)
    key_rows = held[3][...]
    value_rows = held[4][...]
    for chip in range(CHIPS):
        send[chip, 0:PAGE, :] = key_rows
        send[chip, PAGE:KV_ROWS, :] = value_rows
        for chunk in range(CHUNKS):
            send[chip, KV_ROWS + OWN * chunk : KV_ROWS + OWN * (chunk + 1), :] = normed[
                :, LANES * chunk : LANES * (chunk + 1)
            ]


def gathered_tokens(tokens):
    pieces = []
    for chunk in range(CHUNKS):
        first = KV_ROWS + OWN * chunk
        pieces.append(tokens[:, first : first + OWN, :].astype(F32).reshape(LANES, LANES).astype(BF16))
    return jnp.concatenate(pieces, axis=1)


def project_keyvalue(tokens, weights, keyvalue):
    narrow = jnp.concatenate(
        [
            jnp.concatenate([weights[core, chunk, HALF:WEIGHT_ROWS, :].astype(F32) for core in range(CORES)], axis=0)
            for chunk in range(CHUNKS)
        ],
        axis=1,
    ).astype(BF16)
    rounded = dot_nt(narrow, gathered_tokens(tokens)).astype(BF16)
    for place in range(CHIPS * CORES):
        keyvalue[place] = rounded


def project_queries(tokens, weights):
    square = jnp.concatenate(
        [
            jnp.concatenate([weights[core, chunk, 0:HALF, :] for core in range(CORES)], axis=0)
            for chunk in range(CHUNKS)
        ],
        axis=1,
    )
    return dot_nt(gathered_tokens(tokens), square).astype(BF16)


def new_columns(keyvalue, core, first):
    return jnp.concatenate([keyvalue[CORES * chip + core] for chip in range(first, first + CHIPS // 2)], axis=0)


def token_of(index, core):
    chip = ((index >> 3) + FIRST) & (CHIPS - 1)
    return (chip << 4) + OWN * core + (index & 7)


def attend_cached(length_ref, own, weights, keys, values, queries, largest_out, total_out, summed_out):
    length = length_ref[0]
    scale = float(LANES) ** (-0.5)
    query_rows = project_queries(own, weights)
    queries[...] = query_rows
    places = CHIPS * PAGE
    lane = iota((1, places), 1)
    at = (lane * 911) >> 16
    chip = (at + FIRST) & (CHIPS - 1)
    start = lane - PAGE * at + KV_ROWS * chip
    scored = []
    value_sets = []
    for side in range(CORES):
        key_rows = keys[side].astype(F32).reshape(places, LANES).astype(BF16)
        value_sets.append(values[side].astype(F32).reshape(places, LANES).astype(BF16))
        scores = dot_nt(query_rows, key_rows) * scale
        scored.append(jnp.where(start + PAGE * side < length, scores, NEGATIVE))
    largest = jnp.maximum(
        jnp.max(scored[0], axis=1, keepdims=True), jnp.max(scored[1], axis=1, keepdims=True)
    )
    total = jnp.zeros((LANES, 1), F32)
    summed = jnp.zeros((LANES, LANES), F32)
    for scores, value_rows in zip(scored, value_sets):
        terms = jnp.where(scores > 0.5 * NEGATIVE, jnp.exp(scores - largest), 0.0)
        total = total + jnp.sum(terms, axis=1, keepdims=True)
        summed = summed + dot(terms.astype(BF16), value_rows)
    largest_out[...] = jnp.broadcast_to(largest, (LANES, LANES))
    total_out[...] = jnp.broadcast_to(total, (LANES, LANES))
    summed_out[...] = summed


def attend_new(core_ref, queries, old_largest, old_total, old_summed, keyvalue, out_w, result):
    core = core_ref[0]
    scale = float(LANES) ** (-0.5)
    query_rows = queries[...]
    own_token = token_of(iota((LANES, LANES), 0), core)
    scored = []
    for side in range(CORES):
        scores = dot(query_rows, new_columns(keyvalue, side, 0)) * scale
        scored.append(jnp.where(token_of(iota((LANES, LANES), 1), side) <= own_token, scores, NEGATIVE))
    largest = jnp.max(jnp.maximum(scored[0], scored[1]), axis=1, keepdims=True)
    largest = jnp.maximum(old_largest[...], jnp.broadcast_to(largest, (LANES, LANES)))
    factor = jnp.exp(old_largest[...] - largest)
    terms = [jnp.exp(scores - largest) for scores in scored]
    total = old_total[...] * factor + jnp.sum(terms[0] + terms[1], axis=1, keepdims=True)
    summed = old_summed[...] * factor
    for side in range(CORES):
        summed = summed + dot_nt(terms[side].astype(BF16), new_columns(keyvalue, side, CHIPS // 2))
    attended = (summed / total).astype(BF16)
    for chunk in range(0, CHUNKS, 2):
        wide = jnp.concatenate(
            [jnp.concatenate([out_w[0, at], out_w[1, at]], axis=0) for at in (chunk, chunk + 1)], axis=1
        )
        part = dot(attended, wide)
        for at in range(2):
            result[:, OWN * (chunk + at) : OWN * (chunk + at + 1), :] = (
                part[:, LANES * at : LANES * (at + 1)].reshape(CHIPS, OWN, LANES).astype(BF16)
            )


def add_heads(parts, result):
    total = parts[0].astype(F32)
    for chip in range(1, CHIPS):
        total = total + parts[chip].astype(F32)
    for chunk in range(CHUNKS):
        result[:, LANES * chunk : LANES * (chunk + 1)] = total[OWN * chunk : OWN * (chunk + 1), :].astype(BF16)


def write_pages(length_ref, place_ref, keyvalue, key_page, value_page, new_key, new_value):
    length = length_ref[0]
    base = place_ref[0] * PAGE - length
    offset = iota((PAGE, LANES), 0) + base
    inside = (offset >= 0) & (offset < NEW)
    key_rows = jnp.zeros((PAGE, LANES), F32)
    value_rows = jnp.zeros((PAGE, LANES), F32)
    for side in range(CORES):
        chosen = (offset == token_of(iota((PAGE, LANES), 1), side)).astype(F32).astype(BF16)
        key_rows = key_rows + dot_nt(chosen, new_columns(keyvalue, side, 0))
        value_rows = value_rows + dot_nt(chosen, new_columns(keyvalue, side, CHIPS // 2))
    new_key[...] = jnp.where(inside, key_rows, key_page[...].astype(F32)).astype(BF16)
    new_value[...] = jnp.where(inside, value_rows, value_page[...].astype(F32)).astype(BF16)


def call(kernel, shapes, arguments, scalars=0, held=None):
    space = pltpu.VMEM if held is None else pltpu.HBM
    specs = [
        pl.BlockSpec(memory_space=pltpu.SMEM if at < scalars else space) for at in range(len(arguments))
    ]
    scratch = []
    if held is not None:
        scratch = [pltpu.VMEM(shape, dtype) for shape, dtype in held]
        scratch.append(pltpu.SemaphoreType.DMA((len(arguments),)))
    if held is not None:
        arguments = [pltpu.with_memory_space_constraint(argument, pltpu.HBM) for argument in arguments]
    return pl.pallas_call(
        kernel,
        out_shape=[jax.ShapeDtypeStruct(shape, dtype) for shape, dtype in shapes],
        in_specs=specs,
        out_specs=[pl.BlockSpec(memory_space=pltpu.VMEM)] * len(shapes),
        scratch_shapes=scratch,
        compiler_params=pltpu.CompilerParams(vmem_limit_bytes=48 * 1024 * 1024),
    )(*arguments)


def body(
    hidden_states,
    norm_gain,
    norm_bias,
    query_weight,
    keyvalue_weight,
    out_weight,
    key_cache,
    value_cache,
    cache_length,
):
    place = lax.axis_index("gx").astype(jnp.int32).reshape(1)
    core = place & 1
    send, weights = call(
        prepare,
        [((CHIPS, SEND_ROWS, LANES), BF16), ((WEIGHT_ROWS + HALF, LANES), BF16)],
        (
            hidden_states[0],
            norm_gain.reshape(1, FEATURES),
            norm_bias.reshape(1, FEATURES),
            query_weight.T,
            keyvalue_weight.T,
            out_weight,
            key_cache[0],
            value_cache[0],
        ),
        held=[
            ((OWN, FEATURES), BF16),
            ((1, FEATURES), F32),
            ((1, FEATURES), F32),
            ((PAGE, LANES), BF16),
            ((PAGE, LANES), BF16),
        ],
    )
    own = lax.all_to_all(send, "gx", 0, 0, tiled=True, axis_index_groups=SAME_CORE)
    planes = lax.all_gather(weights, "gy", axis=0, tiled=False)
    own, planes = lax.optimization_barrier((own, planes))
    inner = lax.all_gather(planes[:, :WEIGHT_ROWS], "gx", axis=0, tiled=False, axis_index_groups=ONE_CHIP)
    (rows,) = call(project_keyvalue, [((CHIPS * CORES, CORES * OWN, LANES), BF16)], (own, inner))
    own, inner, planes, rows, length = lax.optimization_barrier((own, inner, planes, rows, cache_length))
    keyvalue = lax.all_to_all(rows, "gx", 0, 0, tiled=True)
    keys = lax.all_gather(own[:, :PAGE], "gx", axis=0, tiled=False, axis_index_groups=ONE_CHIP)
    values = lax.all_gather(own[:, PAGE:KV_ROWS], "gx", axis=0, tiled=False, axis_index_groups=ONE_CHIP)
    outer = lax.all_gather(planes[:, WEIGHT_ROWS:], "gx", axis=0, tiled=False, axis_index_groups=ONE_CHIP)
    queries, largest, total, summed = call(
        attend_cached,
        [((LANES, LANES), BF16)] + [((LANES, LANES), F32)] * 3,
        (length, own, inner, keys, values),
        scalars=1,
    )
    keyvalue, outer, summed = lax.optimization_barrier((keyvalue, outer, summed))
    (parts,) = call(
        attend_new,
        [((CHIPS, LANES, LANES), BF16)],
        (core, queries, largest, total, summed, keyvalue, outer),
        scalars=1,
    )
    collected = lax.all_to_all(parts, "gx", 0, 0, tiled=True, axis_index_groups=SAME_CORE)
    new_key, new_value = call(
        write_pages,
        [((PAGE, LANES), BF16), ((PAGE, LANES), BF16)],
        (length, place, keyvalue, key_cache[0], value_cache[0]),
        scalars=2,
    )
    (out,) = call(add_heads, [((OWN, FEATURES), BF16)], (collected,))
    return (out[None], new_key[None], new_value[None])


def solution(mesh):
    return jax.shard_map(
        body,
        mesh=mesh,
        in_specs=(
            P("gy", "gx", None),
            P(),
            P(),
            P("gy", "gx"),
            P("gy", "gx"),
            P("gx", "gy"),
            P("gy", "gx", None),
            P("gy", "gx", None),
            P("gy"),
        ),
        out_specs=(P("gy", "gx", None), P("gy", "gx", None), P("gy", "gx", None)),
        check_vma=False,
    )
```

```python
import jax
import jax.numpy as jnp
from jax import lax
from jax.experimental import pallas as pl
from jax.experimental.pallas import tpu as pltpu
from jax.sharding import PartitionSpec as P

CHIPS = 16
CORES = 2
LANES = 128
HALF = 64
PAGE = 72
OWN = 8
FEATURES = 2048
CHUNKS = FEATURES // LANES
KV_ROWS = 2 * PAGE
SEND_ROWS = KV_ROWS + OWN * CHUNKS
WEIGHT_ROWS = HALF + OWN
NEW = 256
NEGATIVE = -1e30

FIRST = 10
SAME_CORE = [[CORES * ((at + FIRST) % CHIPS) + core for at in range(CHIPS)] for core in range(CORES)]
COLUMNS = [
    [(CORES * chip + (odd + plane) % CORES) * CHUNKS + plane for plane in reversed(range(CHUNKS))]
    for chip in range(CHIPS)
    for odd in range(CORES)
]
ONE_CHIP = [[CORES * chip + core for core in range(CORES)] for chip in range(CHIPS)]
SWAP = [(place, place ^ 1) for place in range(CHIPS * CORES)]

F32 = jnp.float32
BF16 = jnp.bfloat16


def dot(a, b):
    return lax.dot_general(a, b, (((1,), (0,)), ((), ())), preferred_element_type=F32)


def dot_nt(a, b):
    return lax.dot_general(a, b, (((1,), (1,)), ((), ())), preferred_element_type=F32)


def iota(shape, dim):
    return lax.broadcasted_iota(jnp.int32, shape, dim)


def prepare(hidden, gain, bias, query_w, keyvalue_w, out_w, key_page, value_page, send, weights, *scratch):
    held, done = scratch[:-1], scratch[-1]
    targets = held + (
        weights.at[0:HALF],
        weights.at[HALF:WEIGHT_ROWS],
        weights.at[WEIGHT_ROWS : WEIGHT_ROWS + HALF],
    )
    sources = (hidden, gain, bias, key_page, value_page, query_w, keyvalue_w, out_w)
    copies = [
        pltpu.make_async_copy(source, target, done.at[at])
        for at, (source, target) in enumerate(zip(sources, targets))
    ]
    for copy in copies:
        copy.start()
    for copy in copies:
        copy.wait()
    values = held[0][...].astype(F32)
    average = jnp.mean(values, axis=-1, keepdims=True)
    centred = values - average
    spread = jnp.mean(centred * centred, axis=-1, keepdims=True)
    normed = (centred * lax.rsqrt(spread + 1e-05) * held[1][...] + held[2][...]).astype(BF16)
    key_rows = held[3][...]
    value_rows = held[4][...]
    for chip in range(CHIPS):
        send[chip, 0:PAGE, :] = key_rows
        send[chip, PAGE:KV_ROWS, :] = value_rows
        for chunk in range(CHUNKS):
            send[chip, KV_ROWS + OWN * chunk : KV_ROWS + OWN * (chunk + 1), :] = normed[
                :, LANES * chunk : LANES * (chunk + 1)
            ]


def part_of(gathered, odd, core, chunk):
    side = odd if (core + chunk) % CORES == 0 else 1 - odd
    return gathered.at[side, CHUNKS - 1 - chunk]


def gathered_tokens(tokens):
    pieces = []
    for chunk in range(CHUNKS):
        first = KV_ROWS + OWN * chunk
        pieces.append(tokens[:, first : first + OWN, :].astype(F32).reshape(LANES, LANES).astype(BF16))
    return jnp.concatenate(pieces, axis=1)


def project_keyvalue(odd_ref, tokens, weights, keyvalue):
    odd = odd_ref[0]
    narrow = jnp.concatenate(
        [
            jnp.concatenate(
                [part_of(weights, odd, core, chunk)[HALF:WEIGHT_ROWS, :].astype(F32) for core in range(CORES)], axis=0
            )
            for chunk in range(CHUNKS)
        ],
        axis=1,
    ).astype(BF16)
    rounded = dot_nt(narrow, gathered_tokens(tokens)).astype(BF16)
    for place in range(CHIPS * CORES):
        keyvalue[place] = rounded


def project_queries(odd, tokens, weights):
    square = jnp.concatenate(
        [
            jnp.concatenate([part_of(weights, odd, core, chunk)[0:HALF, :] for core in range(CORES)], axis=0)
            for chunk in range(CHUNKS)
        ],
        axis=1,
    )
    return dot_nt(gathered_tokens(tokens), square).astype(BF16)


def new_columns(keyvalue, core, first):
    return jnp.concatenate([keyvalue[CORES * chip + core] for chip in range(first, first + CHIPS // 2)], axis=0)


def token_of(index, core):
    chip = ((index >> 3) + FIRST) & (CHIPS - 1)
    return (chip << 4) + OWN * core + (index & 7)


def attend_cached(length_ref, odd_ref, own, weights, keys, values, queries, largest_out, total_out, summed_out):
    length = length_ref[0]
    scale = float(LANES) ** (-0.5)
    query_rows = project_queries(odd_ref[0], own, weights)
    queries[...] = query_rows
    places = CHIPS * PAGE
    lane = iota((1, places), 1)
    at = (lane * 911) >> 16
    chip = (at + FIRST) & (CHIPS - 1)
    start = lane - PAGE * at + KV_ROWS * chip
    scored = []
    value_sets = []
    for side in range(CORES):
        key_rows = keys[side].astype(F32).reshape(places, LANES).astype(BF16)
        value_sets.append(values[side].astype(F32).reshape(places, LANES).astype(BF16))
        scores = dot_nt(query_rows, key_rows) * scale
        scored.append(jnp.where(start + PAGE * side < length, scores, NEGATIVE))
    largest = jnp.maximum(
        jnp.max(scored[0], axis=1, keepdims=True), jnp.max(scored[1], axis=1, keepdims=True)
    )
    total = jnp.zeros((LANES, 1), F32)
    summed = jnp.zeros((LANES, LANES), F32)
    for scores, value_rows in zip(scored, value_sets):
        terms = jnp.where(scores > 0.5 * NEGATIVE, jnp.exp(scores - largest), 0.0)
        total = total + jnp.sum(terms, axis=1, keepdims=True)
        summed = summed + dot(terms.astype(BF16), value_rows)
    largest_out[...] = jnp.broadcast_to(largest, (LANES, LANES))
    total_out[...] = jnp.broadcast_to(total, (LANES, LANES))
    summed_out[...] = summed


def attend_new(core_ref, odd_ref, queries, old_largest, old_total, old_summed, keyvalue, out_w, result):
    core = core_ref[0]
    scale = float(LANES) ** (-0.5)
    query_rows = queries[...]
    own_token = token_of(iota((LANES, LANES), 0), core)
    scored = []
    for side in range(CORES):
        scores = dot(query_rows, new_columns(keyvalue, side, 0)) * scale
        scored.append(jnp.where(token_of(iota((LANES, LANES), 1), side) <= own_token, scores, NEGATIVE))
    largest = jnp.max(jnp.maximum(scored[0], scored[1]), axis=1, keepdims=True)
    largest = jnp.maximum(old_largest[...], jnp.broadcast_to(largest, (LANES, LANES)))
    factor = jnp.exp(old_largest[...] - largest)
    terms = [jnp.exp(scores - largest) for scores in scored]
    total = old_total[...] * factor + jnp.sum(terms[0] + terms[1], axis=1, keepdims=True)
    summed = old_summed[...] * factor
    for side in range(CORES):
        summed = summed + dot_nt(terms[side].astype(BF16), new_columns(keyvalue, side, CHIPS // 2))
    attended = (summed / total).astype(BF16)
    odd = odd_ref[0]
    for chunk in range(0, CHUNKS, 2):
        wide = jnp.concatenate(
            [
                jnp.concatenate([part_of(out_w, odd, half, at)[...] for half in range(CORES)], axis=0)
                for at in (chunk, chunk + 1)
            ],
            axis=1,
        )
        part = dot(attended, wide)
        for at in range(2):
            result[:, OWN * (chunk + at) : OWN * (chunk + at + 1), :] = (
                part[:, LANES * at : LANES * (at + 1)].reshape(CHIPS, OWN, LANES).astype(BF16)
            )


def add_heads(parts, result):
    total = parts[0].astype(F32)
    for chip in range(1, CHIPS):
        total = total + parts[chip].astype(F32)
    for chunk in range(CHUNKS):
        result[:, LANES * chunk : LANES * (chunk + 1)] = total[OWN * chunk : OWN * (chunk + 1), :].astype(BF16)


def write_pages(length_ref, place_ref, keyvalue, key_page, value_page, new_key, new_value):
    length = length_ref[0]
    base = place_ref[0] * PAGE - length
    offset = iota((PAGE, LANES), 0) + base
    inside = (offset >= 0) & (offset < NEW)
    key_rows = jnp.zeros((PAGE, LANES), F32)
    value_rows = jnp.zeros((PAGE, LANES), F32)
    for side in range(CORES):
        chosen = (offset == token_of(iota((PAGE, LANES), 1), side)).astype(F32).astype(BF16)
        key_rows = key_rows + dot_nt(chosen, new_columns(keyvalue, side, 0))
        value_rows = value_rows + dot_nt(chosen, new_columns(keyvalue, side, CHIPS // 2))
    new_key[...] = jnp.where(inside, key_rows, key_page[...].astype(F32)).astype(BF16)
    new_value[...] = jnp.where(inside, value_rows, value_page[...].astype(F32)).astype(BF16)


def call(kernel, shapes, arguments, scalars=0, held=None):
    space = pltpu.VMEM if held is None else pltpu.HBM
    specs = [
        pl.BlockSpec(memory_space=pltpu.SMEM if at < scalars else space) for at in range(len(arguments))
    ]
    scratch = []
    if held is not None:
        scratch = [pltpu.VMEM(shape, dtype) for shape, dtype in held]
        scratch.append(pltpu.SemaphoreType.DMA((len(arguments),)))
    if held is not None:
        arguments = [pltpu.with_memory_space_constraint(argument, pltpu.HBM) for argument in arguments]
    return pl.pallas_call(
        kernel,
        out_shape=[jax.ShapeDtypeStruct(shape, dtype) for shape, dtype in shapes],
        in_specs=specs,
        out_specs=[pl.BlockSpec(memory_space=pltpu.VMEM)] * len(shapes),
        scratch_shapes=scratch,
        compiler_params=pltpu.CompilerParams(vmem_limit_bytes=48 * 1024 * 1024),
    )(*arguments)


def body(
    hidden_states,
    norm_gain,
    norm_bias,
    query_weight,
    keyvalue_weight,
    out_weight,
    key_cache,
    value_cache,
    cache_length,
):
    place = lax.axis_index("gx").astype(jnp.int32).reshape(1)
    core = place & 1
    odd = lax.axis_index("gy").astype(jnp.int32).reshape(1) & 1
    send, weights = call(
        prepare,
        [((CHIPS, SEND_ROWS, LANES), BF16), ((WEIGHT_ROWS + HALF, LANES), BF16)],
        (
            hidden_states[0],
            norm_gain.reshape(1, FEATURES),
            norm_bias.reshape(1, FEATURES),
            query_weight.T,
            keyvalue_weight.T,
            out_weight,
            key_cache[0],
            value_cache[0],
        ),
        held=[
            ((OWN, FEATURES), BF16),
            ((1, FEATURES), F32),
            ((1, FEATURES), F32),
            ((PAGE, LANES), BF16),
            ((PAGE, LANES), BF16),
        ],
    )
    own = lax.all_to_all(send, "gx", 0, 0, tiled=True, axis_index_groups=SAME_CORE)
    planes = lax.all_gather(weights, ("gx", "gy"), axis=0, tiled=False, axis_index_groups=COLUMNS)
    own, planes = lax.optimization_barrier((own, planes))
    inner = lax.all_gather(planes[:, :WEIGHT_ROWS], "gx", axis=0, tiled=False, axis_index_groups=ONE_CHIP)
    (rows,) = call(project_keyvalue, [((CHIPS * CORES, CORES * OWN, LANES), BF16)], (odd, own, inner), scalars=1)
    own, inner, planes, rows, length = lax.optimization_barrier((own, inner, planes, rows, cache_length))
    keyvalue = lax.all_to_all(rows, "gx", 0, 0, tiled=True)
    keys = lax.all_gather(own[:, :PAGE], "gx", axis=0, tiled=False, axis_index_groups=ONE_CHIP)
    values = lax.all_gather(own[:, PAGE:KV_ROWS], "gx", axis=0, tiled=False, axis_index_groups=ONE_CHIP)
    outer = lax.all_gather(planes[:, WEIGHT_ROWS:], "gx", axis=0, tiled=False, axis_index_groups=ONE_CHIP)
    queries, largest, total, summed = call(
        attend_cached,
        [((LANES, LANES), BF16)] + [((LANES, LANES), F32)] * 3,
        (length, odd, own, inner, keys, values),
        scalars=2,
    )
    keyvalue, outer, summed = lax.optimization_barrier((keyvalue, outer, summed))
    (parts,) = call(
        attend_new,
        [((CHIPS, LANES, LANES), BF16)],
        (core, odd, queries, largest, total, summed, keyvalue, outer),
        scalars=2,
    )
    collected = lax.all_to_all(parts, "gx", 0, 0, tiled=True, axis_index_groups=SAME_CORE)
    new_key, new_value = call(
        write_pages,
        [((PAGE, LANES), BF16), ((PAGE, LANES), BF16)],
        (length, place, keyvalue, key_cache[0], value_cache[0]),
        scalars=2,
    )
    (out,) = call(add_heads, [((OWN, FEATURES), BF16)], (collected,))
    return (out[None], new_key[None], new_value[None])


def solution(mesh):
    return jax.shard_map(
        body,
        mesh=mesh,
        in_specs=(
            P("gy", "gx", None),
            P(),
            P(),
            P("gy", "gx"),
            P("gy", "gx"),
            P("gx", "gy"),
            P("gy", "gx", None),
            P("gy", "gx", None),
            P("gy"),
        ),
        out_specs=(P("gy", "gx", None), P("gy", "gx", None), P("gy", "gx", None)),
        check_vma=False,
    )
```

```python
import jax
import jax.numpy as jnp
from jax import lax
from jax.experimental import pallas as pl
from jax.experimental.pallas import tpu as pltpu
from jax.sharding import PartitionSpec as P

CHIPS = 16
CORES = 2
LANES = 128
HALF = 64
PAGE = 72
OWN = 8
FEATURES = 2048
CHUNKS = FEATURES // LANES
KV_ROWS = 2 * PAGE
SEND_ROWS = KV_ROWS + OWN * CHUNKS
WEIGHT_ROWS = HALF + OWN
NEW = 256
NEGATIVE = -1e30

FIRST = 10
SAME_CORE = [[CORES * ((at + FIRST) % CHIPS) + core for at in range(CHIPS)] for core in range(CORES)]
COLUMNS = [
    [(CORES * chip + (odd + plane) % CORES) * CHUNKS + plane for plane in reversed(range(CHUNKS))]
    for chip in range(CHIPS)
    for odd in range(CORES)
]
ONE_CHIP = [[CORES * chip + core for core in range(CORES)] for chip in range(CHIPS)]
SWAP = [(place, place ^ 1) for place in range(CHIPS * CORES)]

F32 = jnp.float32
BF16 = jnp.bfloat16


def dot(a, b):
    return lax.dot_general(a, b, (((1,), (0,)), ((), ())), preferred_element_type=F32)


def dot_nt(a, b):
    return lax.dot_general(a, b, (((1,), (1,)), ((), ())), preferred_element_type=F32)


def iota(shape, dim):
    return lax.broadcasted_iota(jnp.int32, shape, dim)


def prepare(hidden, gain, bias, query_w, keyvalue_w, out_w, key_page, value_page, send, weights, *scratch):
    held, done = scratch[:-1], scratch[-1]
    targets = held + (
        weights.at[0:HALF],
        weights.at[HALF:WEIGHT_ROWS],
        weights.at[WEIGHT_ROWS : WEIGHT_ROWS + HALF],
    )
    sources = (hidden, gain, bias, key_page, value_page, query_w, keyvalue_w, out_w)
    copies = [
        pltpu.make_async_copy(source, target, done.at[at])
        for at, (source, target) in enumerate(zip(sources, targets))
    ]
    for copy in copies:
        copy.start()
    for copy in copies:
        copy.wait()
    values = held[0][...].astype(F32)
    average = jnp.mean(values, axis=-1, keepdims=True)
    centred = values - average
    spread = jnp.mean(centred * centred, axis=-1, keepdims=True)
    normed = (centred * lax.rsqrt(spread + 1e-05) * held[1][...] + held[2][...]).astype(BF16)
    key_rows = held[3][...]
    value_rows = held[4][...]
    for chip in range(CHIPS):
        send[chip, 0:PAGE, :] = key_rows
        send[chip, PAGE:KV_ROWS, :] = value_rows
        for chunk in range(CHUNKS):
            send[chip, KV_ROWS + OWN * chunk : KV_ROWS + OWN * (chunk + 1), :] = normed[
                :, LANES * chunk : LANES * (chunk + 1)
            ]


def part_of(gathered, odd, core, chunk):
    side = odd if (core + chunk) % CORES == 0 else 1 - odd
    return gathered.at[side, CHUNKS - 1 - chunk]


def gathered_tokens(tokens):
    pieces = []
    for chunk in range(CHUNKS):
        first = KV_ROWS + OWN * chunk
        pieces.append(tokens[:, first : first + OWN, :].astype(F32).reshape(LANES, LANES).astype(BF16))
    return jnp.concatenate(pieces, axis=1)


def project_keyvalue(odd_ref, tokens, weights, planes, keyvalue, swapped):
    odd = odd_ref[0]
    narrow = jnp.concatenate(
        [
            jnp.concatenate(
                [part_of(weights, odd, core, chunk)[HALF:WEIGHT_ROWS, :].astype(F32) for core in range(CORES)], axis=0
            )
            for chunk in range(CHUNKS)
        ],
        axis=1,
    ).astype(BF16)
    rounded = dot_nt(narrow, gathered_tokens(tokens)).astype(BF16)
    for place in range(CHIPS * CORES):
        keyvalue[place] = rounded
    swapped[:, 0:KV_ROWS, :] = tokens[:, 0:KV_ROWS, :]
    swapped[:, KV_ROWS : KV_ROWS + HALF, :] = planes[:, WEIGHT_ROWS : WEIGHT_ROWS + HALF, :]


def project_queries(odd, tokens, weights):
    square = jnp.concatenate(
        [
            jnp.concatenate([part_of(weights, odd, core, chunk)[0:HALF, :] for core in range(CORES)], axis=0)
            for chunk in range(CHUNKS)
        ],
        axis=1,
    )
    return dot_nt(gathered_tokens(tokens), square).astype(BF16)


def new_columns(keyvalue, core, first):
    return jnp.concatenate([keyvalue[CORES * chip + core] for chip in range(first, first + CHIPS // 2)], axis=0)


def token_of(index, core):
    chip = ((index >> 3) + FIRST) & (CHIPS - 1)
    return (chip << 4) + OWN * core + (index & 7)


def attend_cached(
    length_ref, odd_ref, core_ref, own, weights, peer, queries, largest_out, total_out, summed_out
):
    length = length_ref[0]
    core = core_ref[0]
    scale = float(LANES) ** (-0.5)
    query_rows = project_queries(odd_ref[0], own, weights)
    queries[...] = query_rows
    places = CHIPS * PAGE
    lane = iota((1, places), 1)
    at = (lane * 911) >> 16
    chip = (at + FIRST) & (CHIPS - 1)
    start = lane - PAGE * at + KV_ROWS * chip
    scored = []
    value_sets = []
    for source, side in ((own, core), (peer, 1 - core)):
        key_rows = source[:, 0:PAGE, :].astype(F32).reshape(places, LANES).astype(BF16)
        value_sets.append(source[:, PAGE:KV_ROWS, :].astype(F32).reshape(places, LANES).astype(BF16))
        scores = dot_nt(query_rows, key_rows) * scale
        scored.append(jnp.where(start + PAGE * side < length, scores, NEGATIVE))
    largest = jnp.maximum(
        jnp.max(scored[0], axis=1, keepdims=True), jnp.max(scored[1], axis=1, keepdims=True)
    )
    total = jnp.zeros((LANES, 1), F32)
    summed = jnp.zeros((LANES, LANES), F32)
    for scores, value_rows in zip(scored, value_sets):
        terms = jnp.where(scores > 0.5 * NEGATIVE, jnp.exp(scores - largest), 0.0)
        total = total + jnp.sum(terms, axis=1, keepdims=True)
        summed = summed + dot(terms.astype(BF16), value_rows)
    largest_out[...] = jnp.broadcast_to(largest, (LANES, LANES))
    total_out[...] = jnp.broadcast_to(total, (LANES, LANES))
    summed_out[...] = summed


def attend_new(core_ref, odd_ref, queries, old_largest, old_total, old_summed, keyvalue, planes, peer, result):
    core = core_ref[0]
    scale = float(LANES) ** (-0.5)
    query_rows = queries[...]
    own_token = token_of(iota((LANES, LANES), 0), core)
    scored = []
    for side in range(CORES):
        scores = dot(query_rows, new_columns(keyvalue, side, 0)) * scale
        scored.append(jnp.where(token_of(iota((LANES, LANES), 1), side) <= own_token, scores, NEGATIVE))
    largest = jnp.max(jnp.maximum(scored[0], scored[1]), axis=1, keepdims=True)
    largest = jnp.maximum(old_largest[...], jnp.broadcast_to(largest, (LANES, LANES)))
    factor = jnp.exp(old_largest[...] - largest)
    terms = [jnp.exp(scores - largest) for scores in scored]
    total = old_total[...] * factor + jnp.sum(terms[0] + terms[1], axis=1, keepdims=True)
    summed = old_summed[...] * factor
    for side in range(CORES):
        summed = summed + dot_nt(terms[side].astype(BF16), new_columns(keyvalue, side, CHIPS // 2))
    attended = summed / total
    turned = pltpu.roll(attended, HALF, 1)
    same = (core + odd_ref[0]) % CORES == 0
    sides = (jnp.where(same, attended, turned).astype(BF16), jnp.where(same, turned, attended).astype(BF16))
    for chunk in range(CHUNKS):
        at = CHUNKS - 1 - chunk
        square = jnp.concatenate(
            [planes[at, WEIGHT_ROWS : WEIGHT_ROWS + HALF, :], peer[at, KV_ROWS : KV_ROWS + HALF, :]], axis=0
        )
        part = dot(sides[chunk % 2], square)
        result[:, OWN * chunk : OWN * (chunk + 1), :] = part.reshape(CHIPS, OWN, LANES).astype(BF16)


def add_heads(parts, result):
    total = parts[0].astype(F32)
    for chip in range(1, CHIPS):
        total = total + parts[chip].astype(F32)
    for chunk in range(CHUNKS):
        result[:, LANES * chunk : LANES * (chunk + 1)] = total[OWN * chunk : OWN * (chunk + 1), :].astype(BF16)


def write_pages(length_ref, place_ref, keyvalue, key_page, value_page, new_key, new_value):
    length = length_ref[0]
    base = place_ref[0] * PAGE - length
    offset = iota((PAGE, LANES), 0) + base
    inside = (offset >= 0) & (offset < NEW)
    key_rows = jnp.zeros((PAGE, LANES), F32)
    value_rows = jnp.zeros((PAGE, LANES), F32)
    for side in range(CORES):
        chosen = (offset == token_of(iota((PAGE, LANES), 1), side)).astype(F32).astype(BF16)
        key_rows = key_rows + dot_nt(chosen, new_columns(keyvalue, side, 0))
        value_rows = value_rows + dot_nt(chosen, new_columns(keyvalue, side, CHIPS // 2))
    new_key[...] = jnp.where(inside, key_rows, key_page[...].astype(F32)).astype(BF16)
    new_value[...] = jnp.where(inside, value_rows, value_page[...].astype(F32)).astype(BF16)


def call(kernel, shapes, arguments, scalars=0, held=None):
    space = pltpu.VMEM if held is None else pltpu.HBM
    specs = [
        pl.BlockSpec(memory_space=pltpu.SMEM if at < scalars else space) for at in range(len(arguments))
    ]
    scratch = []
    if held is not None:
        scratch = [pltpu.VMEM(shape, dtype) for shape, dtype in held]
        scratch.append(pltpu.SemaphoreType.DMA((len(arguments),)))
    if held is not None:
        arguments = [pltpu.with_memory_space_constraint(argument, pltpu.HBM) for argument in arguments]
    return pl.pallas_call(
        kernel,
        out_shape=[jax.ShapeDtypeStruct(shape, dtype) for shape, dtype in shapes],
        in_specs=specs,
        out_specs=[pl.BlockSpec(memory_space=pltpu.VMEM)] * len(shapes),
        scratch_shapes=scratch,
        compiler_params=pltpu.CompilerParams(vmem_limit_bytes=48 * 1024 * 1024),
    )(*arguments)


def body(
    hidden_states,
    norm_gain,
    norm_bias,
    query_weight,
    keyvalue_weight,
    out_weight,
    key_cache,
    value_cache,
    cache_length,
):
    place = lax.axis_index("gx").astype(jnp.int32).reshape(1)
    core = place & 1
    odd = lax.axis_index("gy").astype(jnp.int32).reshape(1) & 1
    send, weights = call(
        prepare,
        [((CHIPS, SEND_ROWS, LANES), BF16), ((WEIGHT_ROWS + HALF, LANES), BF16)],
        (
            hidden_states[0],
            norm_gain.reshape(1, FEATURES),
            norm_bias.reshape(1, FEATURES),
            query_weight.T,
            keyvalue_weight.T,
            out_weight,
            key_cache[0],
            value_cache[0],
        ),
        held=[
            ((OWN, FEATURES), BF16),
            ((1, FEATURES), F32),
            ((1, FEATURES), F32),
            ((PAGE, LANES), BF16),
            ((PAGE, LANES), BF16),
        ],
    )
    own = lax.all_to_all(send, "gx", 0, 0, tiled=True, axis_index_groups=SAME_CORE)
    planes = lax.all_gather(weights, ("gx", "gy"), axis=0, tiled=False, axis_index_groups=COLUMNS)
    own, planes = lax.optimization_barrier((own, planes))
    inner = lax.all_gather(planes[:, :WEIGHT_ROWS], "gx", axis=0, tiled=False, axis_index_groups=ONE_CHIP)
    rows, swapped = call(
        project_keyvalue,
        [((CHIPS * CORES, CORES * OWN, LANES), BF16), ((CHIPS, KV_ROWS + HALF, LANES), BF16)],
        (odd, own, inner, planes),
        scalars=1,
    )
    keyvalue = lax.all_to_all(rows, "gx", 0, 0, tiled=True)
    peer = lax.ppermute(swapped, "gx", SWAP)
    queries, largest, total, summed = call(
        attend_cached,
        [((LANES, LANES), BF16)] + [((LANES, LANES), F32)] * 3,
        (cache_length, odd, core, own, inner, peer),
        scalars=3,
    )
    (parts,) = call(
        attend_new,
        [((CHIPS, LANES, LANES), BF16)],
        (core, odd, queries, largest, total, summed, keyvalue, planes, peer),
        scalars=2,
    )
    collected = lax.all_to_all(parts, "gx", 0, 0, tiled=True, axis_index_groups=SAME_CORE)
    new_key, new_value = call(
        write_pages,
        [((PAGE, LANES), BF16), ((PAGE, LANES), BF16)],
        (cache_length, place, keyvalue, key_cache[0], value_cache[0]),
        scalars=2,
    )
    (out,) = call(add_heads, [((OWN, FEATURES), BF16)], (collected,))
    return (out[None], new_key[None], new_value[None])


def solution(mesh):
    return jax.shard_map(
        body,
        mesh=mesh,
        in_specs=(
            P("gy", "gx", None),
            P(),
            P(),
            P("gy", "gx"),
            P("gy", "gx"),
            P("gx", "gy"),
            P("gy", "gx", None),
            P("gy", "gx", None),
            P("gy"),
        ),
        out_specs=(P("gy", "gx", None), P("gy", "gx", None), P("gy", "gx", None)),
        check_vma=False,
    )
```

```python
import jax
import jax.numpy as jnp
from jax import lax
from jax.experimental import pallas as pl
from jax.experimental.pallas import tpu as pltpu
from jax.sharding import PartitionSpec as P

CHIPS = 16
CORES = 2
LANES = 128
HALF = 64
PAGE = 72
OWN = 8
FEATURES = 2048
CHUNKS = FEATURES // LANES
KV_ROWS = 2 * PAGE
SEND_ROWS = KV_ROWS + OWN * CHUNKS
WEIGHT_ROWS = HALF + OWN
NEW = 256
NEGATIVE = -1e30

FIRST = 10
SAME_CORE = [[CORES * ((at + FIRST) % CHIPS) + core for at in range(CHIPS)] for core in range(CORES)]
COLUMNS = [
    [(CORES * chip + (odd + plane) % CORES) * CHUNKS + plane for plane in reversed(range(CHUNKS))]
    for chip in range(CHIPS)
    for odd in range(CORES)
]
ONE_CHIP = [[CORES * chip + core for core in range(CORES)] for chip in range(CHIPS)]
SWAP = [(place, place ^ 1) for place in range(CHIPS * CORES)]

F32 = jnp.float32
BF16 = jnp.bfloat16


def dot(a, b):
    return lax.dot_general(a, b, (((1,), (0,)), ((), ())), preferred_element_type=F32)


def dot_nt(a, b):
    return lax.dot_general(a, b, (((1,), (1,)), ((), ())), preferred_element_type=F32)


def iota(shape, dim):
    return lax.broadcasted_iota(jnp.int32, shape, dim)


def prepare(hidden, gain, bias, query_w, keyvalue_w, out_w, key_page, value_page, send, weights, *scratch):
    tokens, gains, biases, block, arrived, left = scratch
    copies = [
        pltpu.make_async_copy(source, target, arrived.at[at])
        for at, (source, target) in enumerate(
            (
                (hidden, tokens),
                (gain, gains),
                (bias, biases),
                (key_page, block.at[0:PAGE]),
                (value_page, block.at[PAGE:KV_ROWS]),
                (query_w, weights.at[0:HALF]),
                (keyvalue_w, weights.at[HALF:WEIGHT_ROWS]),
                (out_w, weights.at[WEIGHT_ROWS : WEIGHT_ROWS + HALF]),
            )
        )
    ]
    for copy in copies:
        copy.start()
    copies[3].wait()
    copies[4].wait()
    sent = [
        pltpu.make_async_copy(block.at[0:KV_ROWS], send.at[chip, 0:KV_ROWS], left.at[chip]) for chip in range(CHIPS)
    ]
    for copy in sent:
        copy.start()
    for copy in copies[:3]:
        copy.wait()
    values = tokens[...].astype(F32)
    average = jnp.mean(values, axis=-1, keepdims=True)
    centred = values - average
    spread = jnp.mean(centred * centred, axis=-1, keepdims=True)
    normed = (centred * lax.rsqrt(spread + 1e-05) * gains[...] + biases[...]).astype(BF16)
    for chunk in range(CHUNKS):
        block[KV_ROWS + OWN * chunk : KV_ROWS + OWN * (chunk + 1), :] = normed[:, LANES * chunk : LANES * (chunk + 1)]
    more = [
        pltpu.make_async_copy(
            block.at[KV_ROWS:SEND_ROWS], send.at[chip, KV_ROWS:SEND_ROWS], left.at[CHIPS + chip]
        )
        for chip in range(CHIPS)
    ]
    for copy in more:
        copy.start()
    for copy in copies[5:] + sent + more:
        copy.wait()


def part_of(gathered, odd, core, chunk):
    side = odd if (core + chunk) % CORES == 0 else 1 - odd
    return gathered.at[side, CHUNKS - 1 - chunk]


def gathered_tokens(tokens):
    pieces = []
    for chunk in range(CHUNKS):
        first = KV_ROWS + OWN * chunk
        pieces.append(tokens[:, first : first + OWN, :].astype(F32).reshape(LANES, LANES).astype(BF16))
    return jnp.concatenate(pieces, axis=1)


def project_keyvalue(odd_ref, tokens, weights, planes, keyvalue, swapped, left):
    copies = [
        pltpu.make_async_copy(tokens.at[:, 0:KV_ROWS], swapped.at[:, 0:KV_ROWS], left.at[0]),
        pltpu.make_async_copy(
            planes.at[:, WEIGHT_ROWS : WEIGHT_ROWS + HALF], swapped.at[:, KV_ROWS : KV_ROWS + HALF], left.at[1]
        ),
    ]
    for copy in copies:
        copy.start()
    odd = odd_ref[0]
    narrow = jnp.concatenate(
        [
            jnp.concatenate(
                [part_of(weights, odd, core, chunk)[HALF:WEIGHT_ROWS, :].astype(F32) for core in range(CORES)], axis=0
            )
            for chunk in range(CHUNKS)
        ],
        axis=1,
    ).astype(BF16)
    rounded = dot_nt(narrow, gathered_tokens(tokens)).astype(BF16)
    for place in range(CHIPS * CORES):
        keyvalue[place] = rounded
    for copy in copies:
        copy.wait()


def project_queries(odd, tokens, weights):
    square = jnp.concatenate(
        [
            jnp.concatenate([part_of(weights, odd, core, chunk)[0:HALF, :] for core in range(CORES)], axis=0)
            for chunk in range(CHUNKS)
        ],
        axis=1,
    )
    return dot_nt(gathered_tokens(tokens), square).astype(BF16)


def new_columns(keyvalue, core, first):
    return jnp.concatenate([keyvalue[CORES * chip + core] for chip in range(first, first + CHIPS // 2)], axis=0)


def token_of(index, core):
    chip = ((index >> 3) + FIRST) & (CHIPS - 1)
    return (chip << 4) + OWN * core + (index & 7)


def attend_cached(
    length_ref, odd_ref, core_ref, own, weights, peer, queries, largest_out, total_out, summed_out
):
    length = length_ref[0]
    core = core_ref[0]
    scale = float(LANES) ** (-0.5)
    query_rows = project_queries(odd_ref[0], own, weights)
    queries[...] = query_rows
    places = CHIPS * PAGE
    lane = iota((1, places), 1)
    at = (lane * 911) >> 16
    chip = (at + FIRST) & (CHIPS - 1)
    start = lane - PAGE * at + KV_ROWS * chip
    scored = []
    value_sets = []
    for source, side in ((own, core), (peer, 1 - core)):
        key_rows = source[:, 0:PAGE, :].astype(F32).reshape(places, LANES).astype(BF16)
        value_sets.append(source[:, PAGE:KV_ROWS, :].astype(F32).reshape(places, LANES).astype(BF16))
        scores = dot_nt(query_rows, key_rows) * scale
        scored.append(jnp.where(start + PAGE * side < length, scores, NEGATIVE))
    largest = jnp.maximum(
        jnp.max(scored[0], axis=1, keepdims=True), jnp.max(scored[1], axis=1, keepdims=True)
    )
    total = jnp.zeros((LANES, 1), F32)
    summed = jnp.zeros((LANES, LANES), F32)
    for scores, value_rows in zip(scored, value_sets):
        terms = jnp.where(scores > 0.5 * NEGATIVE, jnp.exp(scores - largest), 0.0)
        total = total + jnp.sum(terms, axis=1, keepdims=True)
        summed = summed + dot(terms.astype(BF16), value_rows)
    largest_out[...] = jnp.broadcast_to(largest, (LANES, LANES))
    total_out[...] = jnp.broadcast_to(total, (LANES, LANES))
    summed_out[...] = summed


def attend_new(core_ref, odd_ref, queries, old_largest, old_total, old_summed, keyvalue, planes, peer, result):
    core = core_ref[0]
    scale = float(LANES) ** (-0.5)
    query_rows = queries[...]
    own_token = token_of(iota((LANES, LANES), 0), core)
    scored = []
    for side in range(CORES):
        scores = dot(query_rows, new_columns(keyvalue, side, 0)) * scale
        scored.append(jnp.where(token_of(iota((LANES, LANES), 1), side) <= own_token, scores, NEGATIVE))
    largest = jnp.max(jnp.maximum(scored[0], scored[1]), axis=1, keepdims=True)
    largest = jnp.maximum(old_largest[...], jnp.broadcast_to(largest, (LANES, LANES)))
    factor = jnp.exp(old_largest[...] - largest)
    terms = [jnp.exp(scores - largest) for scores in scored]
    total = old_total[...] * factor + jnp.sum(terms[0] + terms[1], axis=1, keepdims=True)
    summed = old_summed[...] * factor
    for side in range(CORES):
        summed = summed + dot_nt(terms[side].astype(BF16), new_columns(keyvalue, side, CHIPS // 2))
    attended = summed / total
    turned = pltpu.roll(attended, HALF, 1)
    same = (core + odd_ref[0]) % CORES == 0
    sides = (jnp.where(same, attended, turned).astype(BF16), jnp.where(same, turned, attended).astype(BF16))
    for parity in range(2):
        chunks = range(parity, CHUNKS, 2)
        wide = jnp.concatenate(
            [
                jnp.concatenate(
                    [
                        planes[CHUNKS - 1 - chunk, WEIGHT_ROWS : WEIGHT_ROWS + HALF, :],
                        peer[CHUNKS - 1 - chunk, KV_ROWS : KV_ROWS + HALF, :],
                    ],
                    axis=0,
                )
                for chunk in chunks
            ],
            axis=1,
        )
        part = dot(sides[parity], wide)
        for at, chunk in enumerate(chunks):
            result[:, OWN * chunk : OWN * (chunk + 1), :] = (
                part[:, LANES * at : LANES * (at + 1)].reshape(CHIPS, OWN, LANES).astype(BF16)
            )


def add_heads(parts, result):
    total = parts[0].astype(F32)
    for chip in range(1, CHIPS):
        total = total + parts[chip].astype(F32)
    for chunk in range(CHUNKS):
        result[:, LANES * chunk : LANES * (chunk + 1)] = total[OWN * chunk : OWN * (chunk + 1), :].astype(BF16)


def write_pages(length_ref, place_ref, keyvalue, key_page, value_page, new_key, new_value):
    length = length_ref[0]
    base = place_ref[0] * PAGE - length
    offset = iota((PAGE, LANES), 0) + base
    inside = (offset >= 0) & (offset < NEW)
    key_rows = jnp.zeros((PAGE, LANES), F32)
    value_rows = jnp.zeros((PAGE, LANES), F32)
    for side in range(CORES):
        chosen = (offset == token_of(iota((PAGE, LANES), 1), side)).astype(F32).astype(BF16)
        key_rows = key_rows + dot_nt(chosen, new_columns(keyvalue, side, 0))
        value_rows = value_rows + dot_nt(chosen, new_columns(keyvalue, side, CHIPS // 2))
    new_key[...] = jnp.where(inside, key_rows, key_page[...].astype(F32)).astype(BF16)
    new_value[...] = jnp.where(inside, value_rows, value_page[...].astype(F32)).astype(BF16)


def call(kernel, shapes, arguments, scalars=0, far=False, spaces=None, scratch=()):
    space = pltpu.HBM if far else pltpu.VMEM
    specs = [
        pl.BlockSpec(memory_space=pltpu.SMEM if at < scalars else space) for at in range(len(arguments))
    ]
    if far:
        arguments = [pltpu.with_memory_space_constraint(argument, pltpu.HBM) for argument in arguments]
    return pl.pallas_call(
        kernel,
        out_shape=[jax.ShapeDtypeStruct(shape, dtype) for shape, dtype in shapes],
        in_specs=specs,
        out_specs=[pl.BlockSpec(memory_space=space) for space in spaces or [pltpu.VMEM] * len(shapes)],
        scratch_shapes=list(scratch),
        compiler_params=pltpu.CompilerParams(vmem_limit_bytes=48 * 1024 * 1024),
    )(*arguments)


def body(
    hidden_states,
    norm_gain,
    norm_bias,
    query_weight,
    keyvalue_weight,
    out_weight,
    key_cache,
    value_cache,
    cache_length,
):
    place = lax.axis_index("gx").astype(jnp.int32).reshape(1)
    core = place & 1
    odd = lax.axis_index("gy").astype(jnp.int32).reshape(1) & 1
    send, weights = call(
        prepare,
        [((CHIPS, SEND_ROWS, LANES), BF16), ((WEIGHT_ROWS + HALF, LANES), BF16)],
        (
            hidden_states[0],
            norm_gain.reshape(1, FEATURES),
            norm_bias.reshape(1, FEATURES),
            query_weight.T,
            keyvalue_weight.T,
            out_weight,
            key_cache[0],
            value_cache[0],
        ),
        far=True,
        spaces=[pltpu.HBM, pltpu.VMEM],
        scratch=[
            pltpu.VMEM((OWN, FEATURES), BF16),
            pltpu.VMEM((1, FEATURES), F32),
            pltpu.VMEM((1, FEATURES), F32),
            pltpu.VMEM((SEND_ROWS, LANES), BF16),
            pltpu.SemaphoreType.DMA((8,)),
            pltpu.SemaphoreType.DMA((2 * CHIPS,)),
        ],
    )
    own = lax.all_to_all(send, "gx", 0, 0, tiled=True, axis_index_groups=SAME_CORE)
    planes = lax.all_gather(weights, ("gx", "gy"), axis=0, tiled=False, axis_index_groups=COLUMNS)
    own, planes = lax.optimization_barrier((own, planes))
    inner = lax.all_gather(planes[:, :WEIGHT_ROWS], "gx", axis=0, tiled=False, axis_index_groups=ONE_CHIP)
    rows, swapped = call(
        project_keyvalue,
        [((CHIPS * CORES, CORES * OWN, LANES), BF16), ((CHIPS, KV_ROWS + HALF, LANES), BF16)],
        (odd, own, inner, planes),
        scalars=1,
        spaces=[pltpu.VMEM, pltpu.HBM],
        scratch=[pltpu.SemaphoreType.DMA((2,))],
    )
    keyvalue = lax.all_to_all(rows, "gx", 0, 0, tiled=True)
    peer = lax.ppermute(swapped, "gx", SWAP)
    queries, largest, total, summed = call(
        attend_cached,
        [((LANES, LANES), BF16)] + [((LANES, LANES), F32)] * 3,
        (cache_length, odd, core, own, inner, peer),
        scalars=3,
    )
    (parts,) = call(
        attend_new,
        [((CHIPS, LANES, LANES), BF16)],
        (core, odd, queries, largest, total, summed, keyvalue, planes, peer),
        scalars=2,
    )
    collected = lax.all_to_all(parts, "gx", 0, 0, tiled=True, axis_index_groups=SAME_CORE)
    new_key, new_value = call(
        write_pages,
        [((PAGE, LANES), BF16), ((PAGE, LANES), BF16)],
        (cache_length, place, keyvalue, key_cache[0], value_cache[0]),
        scalars=2,
    )
    (out,) = call(add_heads, [((OWN, FEATURES), BF16)], (collected,))
    return (out[None], new_key[None], new_value[None])


def solution(mesh):
    return jax.shard_map(
        body,
        mesh=mesh,
        in_specs=(
            P("gy", "gx", None),
            P(),
            P(),
            P("gy", "gx"),
            P("gy", "gx"),
            P("gx", "gy"),
            P("gy", "gx", None),
            P("gy", "gx", None),
            P("gy"),
        ),
        out_specs=(P("gy", "gx", None), P("gy", "gx", None), P("gy", "gx", None)),
        check_vma=False,
    )
```

```python
import jax
import jax.numpy as jnp
from jax import lax
from jax.experimental import pallas as pl
from jax.experimental.pallas import tpu as pltpu
from jax.sharding import PartitionSpec as P

CHIPS = 16
CORES = 2
LANES = 128
HALF = 64
PAGE = 72
OWN = 8
FEATURES = 2048
CHUNKS = FEATURES // LANES
KV_ROWS = 2 * PAGE
SEND_ROWS = KV_ROWS + OWN * CHUNKS
WEIGHT_ROWS = HALF + OWN
NEW = 256
NEGATIVE = -1e30

FIRST = 10
SAME_CORE = [[CORES * ((at + FIRST) % CHIPS) + core for at in range(CHIPS)] for core in range(CORES)]
COLUMNS = [
    [(CORES * chip + (odd + plane) % CORES) * CHUNKS + plane for plane in reversed(range(CHUNKS))]
    for chip in range(CHIPS)
    for odd in range(CORES)
]
ONE_CHIP = [[CORES * chip + core for core in range(CORES)] for chip in range(CHIPS)]
SWAP = [(place, place ^ 1) for place in range(CHIPS * CORES)]

F32 = jnp.float32
BF16 = jnp.bfloat16


def dot(a, b):
    return lax.dot_general(a, b, (((1,), (0,)), ((), ())), preferred_element_type=F32)


def dot_nt(a, b):
    return lax.dot_general(a, b, (((1,), (1,)), ((), ())), preferred_element_type=F32)


def iota(shape, dim):
    return lax.broadcasted_iota(jnp.int32, shape, dim)


def prepare(hidden, gain, bias, query_w, keyvalue_w, out_w, key_page, value_page, send, weights, *scratch):
    held, done = scratch[:-1], scratch[-1]
    targets = held + (
        weights.at[0:HALF],
        weights.at[HALF:WEIGHT_ROWS],
        weights.at[WEIGHT_ROWS : WEIGHT_ROWS + HALF],
    )
    sources = (hidden, gain, bias, key_page, value_page, query_w, keyvalue_w, out_w)
    copies = [
        pltpu.make_async_copy(source, target, done.at[at])
        for at, (source, target) in enumerate(zip(sources, targets))
    ]
    for copy in copies:
        copy.start()
    for copy in copies:
        copy.wait()
    values = held[0][...].astype(F32)
    average = jnp.mean(values, axis=-1, keepdims=True)
    centred = values - average
    spread = jnp.mean(centred * centred, axis=-1, keepdims=True)
    normed = (centred * lax.rsqrt(spread + 1e-05) * held[1][...] + held[2][...]).astype(BF16)
    key_rows = held[3][...]
    value_rows = held[4][...]
    for chip in range(CHIPS):
        send[chip, 0:PAGE, :] = key_rows
        send[chip, PAGE:KV_ROWS, :] = value_rows
        for chunk in range(CHUNKS):
            send[chip, KV_ROWS + OWN * chunk : KV_ROWS + OWN * (chunk + 1), :] = normed[
                :, LANES * chunk : LANES * (chunk + 1)
            ]


def part_of(gathered, odd, core, chunk):
    side = odd if (core + chunk) % CORES == 0 else 1 - odd
    return gathered.at[side, CHUNKS - 1 - chunk]


def gathered_tokens(tokens, chunks=range(CHUNKS)):
    pieces = []
    for chunk in chunks:
        first = KV_ROWS + OWN * chunk
        pieces.append(tokens[:, first : first + OWN, :].astype(F32).reshape(LANES, LANES).astype(BF16))
    return jnp.concatenate(pieces, axis=1)


def project_keyvalue(odd_ref, tokens, weights, planes, keyvalue, swapped):
    odd = odd_ref[0]
    narrow = jnp.concatenate(
        [
            jnp.concatenate(
                [part_of(weights, odd, core, chunk)[...].astype(F32) for core in range(CORES)], axis=0
            )
            for chunk in range(CHUNKS)
        ],
        axis=1,
    ).astype(BF16)
    rounded = dot_nt(narrow, gathered_tokens(tokens)).astype(BF16)
    for place in range(CHIPS * CORES):
        keyvalue[place] = rounded
    swapped[:, 0:KV_ROWS, :] = tokens[:, 0:KV_ROWS, :]
    swapped[:, KV_ROWS : KV_ROWS + HALF, :] = planes[:, WEIGHT_ROWS : WEIGHT_ROWS + HALF, :]
    swapped[:, KV_ROWS + HALF : SEND_ROWS, :] = planes[:, 0:HALF, :]


def project_queries(same, tokens, planes, peer):
    sums = []
    for parity in range(2):
        chunks = range(parity, CHUNKS, 2)
        square = jnp.concatenate(
            [
                jnp.concatenate(
                    [planes[CHUNKS - 1 - chunk, 0:HALF, :], peer[CHUNKS - 1 - chunk, KV_ROWS + HALF : SEND_ROWS, :]],
                    axis=0,
                )
                for chunk in chunks
            ],
            axis=1,
        )
        sums.append(dot_nt(gathered_tokens(tokens, chunks), square))
    total = sums[0] + pltpu.roll(sums[1], HALF, 1)
    return jnp.where(same, total, pltpu.roll(total, HALF, 1)).astype(BF16)


def new_columns(keyvalue, core, first):
    return jnp.concatenate([keyvalue[CORES * chip + core] for chip in range(first, first + CHIPS // 2)], axis=0)


def token_of(index, core):
    chip = ((index >> 3) + FIRST) & (CHIPS - 1)
    return (chip << 4) + OWN * core + (index & 7)


def attend_cached(
    length_ref, odd_ref, core_ref, own, planes, peer, queries, largest_out, total_out, summed_out
):
    length = length_ref[0]
    core = core_ref[0]
    scale = float(LANES) ** (-0.5)
    query_rows = project_queries((core + odd_ref[0]) % CORES == 0, own, planes, peer)
    queries[...] = query_rows
    places = CHIPS * PAGE
    lane = iota((1, places), 1)
    at = (lane * 911) >> 16
    chip = (at + FIRST) & (CHIPS - 1)
    start = lane - PAGE * at + KV_ROWS * chip
    scored = []
    value_sets = []
    for source, side in ((own, core), (peer, 1 - core)):
        key_rows = source[:, 0:PAGE, :].astype(F32).reshape(places, LANES).astype(BF16)
        value_sets.append(source[:, PAGE:KV_ROWS, :].astype(F32).reshape(places, LANES).astype(BF16))
        scores = dot_nt(query_rows, key_rows) * scale
        scored.append(jnp.where(start + PAGE * side < length, scores, NEGATIVE))
    largest = jnp.maximum(
        jnp.max(scored[0], axis=1, keepdims=True), jnp.max(scored[1], axis=1, keepdims=True)
    )
    total = jnp.zeros((LANES, 1), F32)
    summed = jnp.zeros((LANES, LANES), F32)
    for scores, value_rows in zip(scored, value_sets):
        terms = jnp.where(scores > 0.5 * NEGATIVE, jnp.exp(scores - largest), 0.0)
        total = total + jnp.sum(terms, axis=1, keepdims=True)
        summed = summed + dot(terms.astype(BF16), value_rows)
    largest_out[...] = jnp.broadcast_to(largest, (LANES, LANES))
    total_out[...] = jnp.broadcast_to(total, (LANES, LANES))
    summed_out[...] = summed


def attend_new(core_ref, odd_ref, queries, old_largest, old_total, old_summed, keyvalue, planes, peer, result):
    core = core_ref[0]
    scale = float(LANES) ** (-0.5)
    query_rows = queries[...]
    own_token = token_of(iota((LANES, LANES), 0), core)
    scored = []
    for side in range(CORES):
        scores = dot(query_rows, new_columns(keyvalue, side, 0)) * scale
        scored.append(jnp.where(token_of(iota((LANES, LANES), 1), side) <= own_token, scores, NEGATIVE))
    largest = jnp.max(jnp.maximum(scored[0], scored[1]), axis=1, keepdims=True)
    largest = jnp.maximum(old_largest[...], jnp.broadcast_to(largest, (LANES, LANES)))
    factor = jnp.exp(old_largest[...] - largest)
    terms = [jnp.exp(scores - largest) for scores in scored]
    total = old_total[...] * factor + jnp.sum(terms[0] + terms[1], axis=1, keepdims=True)
    summed = old_summed[...] * factor
    for side in range(CORES):
        summed = summed + dot_nt(terms[side].astype(BF16), new_columns(keyvalue, side, CHIPS // 2))
    attended = summed / total
    turned = pltpu.roll(attended, HALF, 1)
    same = (core + odd_ref[0]) % CORES == 0
    sides = (jnp.where(same, attended, turned).astype(BF16), jnp.where(same, turned, attended).astype(BF16))
    for chunk in range(CHUNKS):
        at = CHUNKS - 1 - chunk
        square = jnp.concatenate(
            [planes[at, WEIGHT_ROWS : WEIGHT_ROWS + HALF, :], peer[at, KV_ROWS : KV_ROWS + HALF, :]], axis=0
        )
        part = dot(sides[chunk % 2], square)
        result[:, OWN * chunk : OWN * (chunk + 1), :] = part.reshape(CHIPS, OWN, LANES).astype(BF16)


def add_heads(parts, result):
    total = parts[0].astype(F32)
    for chip in range(1, CHIPS):
        total = total + parts[chip].astype(F32)
    for chunk in range(CHUNKS):
        result[:, LANES * chunk : LANES * (chunk + 1)] = total[OWN * chunk : OWN * (chunk + 1), :].astype(BF16)


def write_pages(length_ref, place_ref, keyvalue, key_page, value_page, new_key, new_value):
    length = length_ref[0]
    base = place_ref[0] * PAGE - length
    offset = iota((PAGE, LANES), 0) + base
    inside = (offset >= 0) & (offset < NEW)
    key_rows = jnp.zeros((PAGE, LANES), F32)
    value_rows = jnp.zeros((PAGE, LANES), F32)
    for side in range(CORES):
        chosen = (offset == token_of(iota((PAGE, LANES), 1), side)).astype(F32).astype(BF16)
        key_rows = key_rows + dot_nt(chosen, new_columns(keyvalue, side, 0))
        value_rows = value_rows + dot_nt(chosen, new_columns(keyvalue, side, CHIPS // 2))
    new_key[...] = jnp.where(inside, key_rows, key_page[...].astype(F32)).astype(BF16)
    new_value[...] = jnp.where(inside, value_rows, value_page[...].astype(F32)).astype(BF16)


def call(kernel, shapes, arguments, scalars=0, held=None):
    space = pltpu.VMEM if held is None else pltpu.HBM
    specs = [
        pl.BlockSpec(memory_space=pltpu.SMEM if at < scalars else space) for at in range(len(arguments))
    ]
    scratch = []
    if held is not None:
        scratch = [pltpu.VMEM(shape, dtype) for shape, dtype in held]
        scratch.append(pltpu.SemaphoreType.DMA((len(arguments),)))
    if held is not None:
        arguments = [pltpu.with_memory_space_constraint(argument, pltpu.HBM) for argument in arguments]
    return pl.pallas_call(
        kernel,
        out_shape=[jax.ShapeDtypeStruct(shape, dtype) for shape, dtype in shapes],
        in_specs=specs,
        out_specs=[pl.BlockSpec(memory_space=pltpu.VMEM)] * len(shapes),
        scratch_shapes=scratch,
        compiler_params=pltpu.CompilerParams(vmem_limit_bytes=48 * 1024 * 1024),
    )(*arguments)


def body(
    hidden_states,
    norm_gain,
    norm_bias,
    query_weight,
    keyvalue_weight,
    out_weight,
    key_cache,
    value_cache,
    cache_length,
):
    place = lax.axis_index("gx").astype(jnp.int32).reshape(1)
    core = place & 1
    odd = lax.axis_index("gy").astype(jnp.int32).reshape(1) & 1
    send, weights = call(
        prepare,
        [((CHIPS, SEND_ROWS, LANES), BF16), ((WEIGHT_ROWS + HALF, LANES), BF16)],
        (
            hidden_states[0],
            norm_gain.reshape(1, FEATURES),
            norm_bias.reshape(1, FEATURES),
            query_weight.T,
            keyvalue_weight.T,
            out_weight,
            key_cache[0],
            value_cache[0],
        ),
        held=[
            ((OWN, FEATURES), BF16),
            ((1, FEATURES), F32),
            ((1, FEATURES), F32),
            ((PAGE, LANES), BF16),
            ((PAGE, LANES), BF16),
        ],
    )
    own = lax.all_to_all(send, "gx", 0, 0, tiled=True, axis_index_groups=SAME_CORE)
    planes = lax.all_gather(weights, ("gx", "gy"), axis=0, tiled=False, axis_index_groups=COLUMNS)
    own, planes = lax.optimization_barrier((own, planes))
    inner = lax.all_gather(planes[:, HALF:WEIGHT_ROWS], "gx", axis=0, tiled=False, axis_index_groups=ONE_CHIP)
    rows, swapped = call(
        project_keyvalue,
        [((CHIPS * CORES, CORES * OWN, LANES), BF16), ((CHIPS, SEND_ROWS, LANES), BF16)],
        (odd, own, inner, planes),
        scalars=1,
    )
    keyvalue = lax.all_to_all(rows, "gx", 0, 0, tiled=True)
    peer = lax.ppermute(swapped, "gx", SWAP)
    queries, largest, total, summed = call(
        attend_cached,
        [((LANES, LANES), BF16)] + [((LANES, LANES), F32)] * 3,
        (cache_length, odd, core, own, planes, peer),
        scalars=3,
    )
    (parts,) = call(
        attend_new,
        [((CHIPS, LANES, LANES), BF16)],
        (core, odd, queries, largest, total, summed, keyvalue, planes, peer),
        scalars=2,
    )
    collected = lax.all_to_all(parts, "gx", 0, 0, tiled=True, axis_index_groups=SAME_CORE)
    new_key, new_value = call(
        write_pages,
        [((PAGE, LANES), BF16), ((PAGE, LANES), BF16)],
        (cache_length, place, keyvalue, key_cache[0], value_cache[0]),
        scalars=2,
    )
    (out,) = call(add_heads, [((OWN, FEATURES), BF16)], (collected,))
    return (out[None], new_key[None], new_value[None])


def solution(mesh):
    return jax.shard_map(
        body,
        mesh=mesh,
        in_specs=(
            P("gy", "gx", None),
            P(),
            P(),
            P("gy", "gx"),
            P("gy", "gx"),
            P("gx", "gy"),
            P("gy", "gx", None),
            P("gy", "gx", None),
            P("gy"),
        ),
        out_specs=(P("gy", "gx", None), P("gy", "gx", None), P("gy", "gx", None)),
        check_vma=False,
    )
```

```python
import jax
import jax.numpy as jnp
from jax import lax
from jax.experimental import pallas as pl
from jax.experimental.pallas import tpu as pltpu
from jax.sharding import PartitionSpec as P

CHIPS = 16
CORES = 2
LANES = 128
HALF = 64
PAGE = 72
OWN = 8
FEATURES = 2048
CHUNKS = FEATURES // LANES
KV_ROWS = 2 * PAGE
SEND_ROWS = KV_ROWS + OWN * CHUNKS
WEIGHT_ROWS = HALF + CORES * OWN
NEW = 256
NEGATIVE = -1e30

FIRST = 10
SAME_CORE = [[CORES * ((at + FIRST) % CHIPS) + core for at in range(CHIPS)] for core in range(CORES)]
COLUMNS = [
    [(CORES * chip + (odd + plane) % CORES) * CHUNKS + plane for plane in reversed(range(CHUNKS))]
    for chip in range(CHIPS)
    for odd in range(CORES)
]
ONE_CHIP = [[CORES * chip + core for core in range(CORES)] for chip in range(CHIPS)]
SWAP = [(place, place ^ 1) for place in range(CHIPS * CORES)]

F32 = jnp.float32
BF16 = jnp.bfloat16


def dot(a, b):
    return lax.dot_general(a, b, (((1,), (0,)), ((), ())), preferred_element_type=F32)


def dot_nt(a, b):
    return lax.dot_general(a, b, (((1,), (1,)), ((), ())), preferred_element_type=F32)


def iota(shape, dim):
    return lax.broadcasted_iota(jnp.int32, shape, dim)


def prepare(hidden, gain, bias, query_w, keyvalue_w, out_w, key_page, value_page, send, weights, *scratch):
    held, done = scratch[:-1], scratch[-1]
    targets = held + (
        weights.at[0:HALF],
        weights.at[HALF:WEIGHT_ROWS],
        weights.at[WEIGHT_ROWS : WEIGHT_ROWS + HALF],
    )
    sources = (hidden, gain, bias, key_page, value_page, query_w, keyvalue_w, out_w)
    copies = [
        pltpu.make_async_copy(source, target, done.at[at])
        for at, (source, target) in enumerate(zip(sources, targets))
    ]
    for copy in copies:
        copy.start()
    for copy in copies:
        copy.wait()
    values = held[0][...].astype(F32)
    average = jnp.mean(values, axis=-1, keepdims=True)
    centred = values - average
    spread = jnp.mean(centred * centred, axis=-1, keepdims=True)
    normed = (centred * lax.rsqrt(spread + 1e-05) * held[1][...] + held[2][...]).astype(BF16)
    key_rows = held[3][...]
    value_rows = held[4][...]
    for chip in range(CHIPS):
        send[chip, 0:PAGE, :] = key_rows
        send[chip, PAGE:KV_ROWS, :] = value_rows
        for chunk in range(CHUNKS):
            send[chip, KV_ROWS + OWN * chunk : KV_ROWS + OWN * (chunk + 1), :] = normed[
                :, LANES * chunk : LANES * (chunk + 1)
            ]


def gathered_tokens(tokens, chunks=range(CHUNKS)):
    pieces = []
    for chunk in chunks:
        first = KV_ROWS + OWN * chunk
        pieces.append(tokens[:, first : first + OWN, :].astype(F32).reshape(LANES, LANES).astype(BF16))
    return jnp.concatenate(pieces, axis=1)


def project_keyvalue(tokens, planes, keyvalue, swapped):
    narrow = jnp.concatenate([planes[CHUNKS - 1 - chunk, HALF:WEIGHT_ROWS, :] for chunk in range(CHUNKS)], axis=1)
    rounded = dot_nt(narrow, gathered_tokens(tokens)).astype(BF16)
    for place in range(CHIPS * CORES):
        keyvalue[place] = rounded
    swapped[:, 0:KV_ROWS, :] = tokens[:, 0:KV_ROWS, :]
    swapped[:, KV_ROWS : KV_ROWS + HALF, :] = planes[:, WEIGHT_ROWS : WEIGHT_ROWS + HALF, :]
    swapped[:, KV_ROWS + HALF : SEND_ROWS, :] = planes[:, 0:HALF, :]


def project_queries(same, tokens, planes, peer):
    sums = []
    for parity in range(2):
        chunks = range(parity, CHUNKS, 2)
        square = jnp.concatenate(
            [
                jnp.concatenate(
                    [planes[CHUNKS - 1 - chunk, 0:HALF, :], peer[CHUNKS - 1 - chunk, KV_ROWS + HALF : SEND_ROWS, :]],
                    axis=0,
                )
                for chunk in chunks
            ],
            axis=1,
        )
        sums.append(dot_nt(gathered_tokens(tokens, chunks), square))
    total = sums[0] + pltpu.roll(sums[1], HALF, 1)
    return jnp.where(same, total, pltpu.roll(total, HALF, 1)).astype(BF16)


def new_columns(keyvalue, core, first):
    return jnp.concatenate([keyvalue[CORES * chip + core] for chip in range(first, first + CHIPS // 2)], axis=0)


def token_of(index, core):
    chip = ((index >> 3) + FIRST) & (CHIPS - 1)
    return (chip << 4) + OWN * core + (index & 7)


def attend_cached(
    length_ref, odd_ref, core_ref, own, planes, peer, queries, largest_out, total_out, summed_out
):
    length = length_ref[0]
    core = core_ref[0]
    scale = float(LANES) ** (-0.5)
    query_rows = project_queries((core + odd_ref[0]) % CORES == 0, own, planes, peer)
    queries[...] = query_rows
    places = CHIPS * PAGE
    lane = iota((1, places), 1)
    at = (lane * 911) >> 16
    chip = (at + FIRST) & (CHIPS - 1)
    start = lane - PAGE * at + KV_ROWS * chip
    scored = []
    value_sets = []
    for source, side in ((own, core), (peer, 1 - core)):
        key_rows = source[:, 0:PAGE, :].astype(F32).reshape(places, LANES).astype(BF16)
        value_sets.append(source[:, PAGE:KV_ROWS, :].astype(F32).reshape(places, LANES).astype(BF16))
        scores = dot_nt(query_rows, key_rows) * scale
        scored.append(jnp.where(start + PAGE * side < length, scores, NEGATIVE))
    largest = jnp.maximum(
        jnp.max(scored[0], axis=1, keepdims=True), jnp.max(scored[1], axis=1, keepdims=True)
    )
    total = jnp.zeros((LANES, 1), F32)
    summed = jnp.zeros((LANES, LANES), F32)
    for scores, value_rows in zip(scored, value_sets):
        terms = jnp.where(scores > 0.5 * NEGATIVE, jnp.exp(scores - largest), 0.0)
        total = total + jnp.sum(terms, axis=1, keepdims=True)
        summed = summed + dot(terms.astype(BF16), value_rows)
    largest_out[...] = jnp.broadcast_to(largest, (LANES, LANES))
    total_out[...] = jnp.broadcast_to(total, (LANES, LANES))
    summed_out[...] = summed


def attend_new(core_ref, odd_ref, queries, old_largest, old_total, old_summed, keyvalue, planes, peer, result):
    core = core_ref[0]
    scale = float(LANES) ** (-0.5)
    query_rows = queries[...]
    own_token = token_of(iota((LANES, LANES), 0), core)
    scored = []
    for side in range(CORES):
        scores = dot(query_rows, new_columns(keyvalue, side, 0)) * scale
        scored.append(jnp.where(token_of(iota((LANES, LANES), 1), side) <= own_token, scores, NEGATIVE))
    largest = jnp.max(jnp.maximum(scored[0], scored[1]), axis=1, keepdims=True)
    largest = jnp.maximum(old_largest[...], jnp.broadcast_to(largest, (LANES, LANES)))
    factor = jnp.exp(old_largest[...] - largest)
    terms = [jnp.exp(scores - largest) for scores in scored]
    total = old_total[...] * factor + jnp.sum(terms[0] + terms[1], axis=1, keepdims=True)
    summed = old_summed[...] * factor
    for side in range(CORES):
        summed = summed + dot_nt(terms[side].astype(BF16), new_columns(keyvalue, side, CHIPS // 2))
    attended = summed / total
    turned = pltpu.roll(attended, HALF, 1)
    same = (core + odd_ref[0]) % CORES == 0
    sides = (jnp.where(same, attended, turned).astype(BF16), jnp.where(same, turned, attended).astype(BF16))
    for chunk in range(CHUNKS):
        at = CHUNKS - 1 - chunk
        square = jnp.concatenate(
            [planes[at, WEIGHT_ROWS : WEIGHT_ROWS + HALF, :], peer[at, KV_ROWS : KV_ROWS + HALF, :]], axis=0
        )
        part = dot(sides[chunk % 2], square)
        result[:, OWN * chunk : OWN * (chunk + 1), :] = part.reshape(CHIPS, OWN, LANES).astype(BF16)


def add_heads(parts, result):
    total = parts[0].astype(F32)
    for chip in range(1, CHIPS):
        total = total + parts[chip].astype(F32)
    for chunk in range(CHUNKS):
        result[:, LANES * chunk : LANES * (chunk + 1)] = total[OWN * chunk : OWN * (chunk + 1), :].astype(BF16)


def write_pages(length_ref, place_ref, keyvalue, key_page, value_page, new_key, new_value):
    length = length_ref[0]
    base = place_ref[0] * PAGE - length
    offset = iota((PAGE, LANES), 0) + base
    inside = (offset >= 0) & (offset < NEW)
    key_rows = jnp.zeros((PAGE, LANES), F32)
    value_rows = jnp.zeros((PAGE, LANES), F32)
    for side in range(CORES):
        chosen = (offset == token_of(iota((PAGE, LANES), 1), side)).astype(F32).astype(BF16)
        key_rows = key_rows + dot_nt(chosen, new_columns(keyvalue, side, 0))
        value_rows = value_rows + dot_nt(chosen, new_columns(keyvalue, side, CHIPS // 2))
    new_key[...] = jnp.where(inside, key_rows, key_page[...].astype(F32)).astype(BF16)
    new_value[...] = jnp.where(inside, value_rows, value_page[...].astype(F32)).astype(BF16)


def call(kernel, shapes, arguments, scalars=0, held=None):
    space = pltpu.VMEM if held is None else pltpu.HBM
    specs = [
        pl.BlockSpec(memory_space=pltpu.SMEM if at < scalars else space) for at in range(len(arguments))
    ]
    scratch = []
    if held is not None:
        scratch = [pltpu.VMEM(shape, dtype) for shape, dtype in held]
        scratch.append(pltpu.SemaphoreType.DMA((len(arguments),)))
    if held is not None:
        arguments = [pltpu.with_memory_space_constraint(argument, pltpu.HBM) for argument in arguments]
    return pl.pallas_call(
        kernel,
        out_shape=[jax.ShapeDtypeStruct(shape, dtype) for shape, dtype in shapes],
        in_specs=specs,
        out_specs=[pl.BlockSpec(memory_space=pltpu.VMEM)] * len(shapes),
        scratch_shapes=scratch,
        compiler_params=pltpu.CompilerParams(vmem_limit_bytes=48 * 1024 * 1024),
    )(*arguments)


def body(
    hidden_states,
    norm_gain,
    norm_bias,
    query_weight,
    keyvalue_weight,
    out_weight,
    key_cache,
    value_cache,
    cache_length,
):
    place = lax.axis_index("gx").astype(jnp.int32).reshape(1)
    core = place & 1
    odd = lax.axis_index("gy").astype(jnp.int32).reshape(1) & 1
    both = lax.all_gather(keyvalue_weight.T, "gx", axis=0, tiled=True, axis_index_groups=ONE_CHIP)
    send, weights = call(
        prepare,
        [((CHIPS, SEND_ROWS, LANES), BF16), ((WEIGHT_ROWS + HALF, LANES), BF16)],
        (
            hidden_states[0],
            norm_gain.reshape(1, FEATURES),
            norm_bias.reshape(1, FEATURES),
            query_weight.T,
            both,
            out_weight,
            key_cache[0],
            value_cache[0],
        ),
        held=[
            ((OWN, FEATURES), BF16),
            ((1, FEATURES), F32),
            ((1, FEATURES), F32),
            ((PAGE, LANES), BF16),
            ((PAGE, LANES), BF16),
        ],
    )
    own = lax.all_to_all(send, "gx", 0, 0, tiled=True, axis_index_groups=SAME_CORE)
    planes = lax.all_gather(weights, ("gx", "gy"), axis=0, tiled=False, axis_index_groups=COLUMNS)
    own, planes = lax.optimization_barrier((own, planes))
    rows, swapped = call(
        project_keyvalue,
        [((CHIPS * CORES, CORES * OWN, LANES), BF16), ((CHIPS, SEND_ROWS, LANES), BF16)],
        (own, planes),
    )
    keyvalue = lax.all_to_all(rows, "gx", 0, 0, tiled=True)
    peer = lax.ppermute(swapped, "gx", SWAP)
    queries, largest, total, summed = call(
        attend_cached,
        [((LANES, LANES), BF16)] + [((LANES, LANES), F32)] * 3,
        (cache_length, odd, core, own, planes, peer),
        scalars=3,
    )
    (parts,) = call(
        attend_new,
        [((CHIPS, LANES, LANES), BF16)],
        (core, odd, queries, largest, total, summed, keyvalue, planes, peer),
        scalars=2,
    )
    collected = lax.all_to_all(parts, "gx", 0, 0, tiled=True, axis_index_groups=SAME_CORE)
    new_key, new_value = call(
        write_pages,
        [((PAGE, LANES), BF16), ((PAGE, LANES), BF16)],
        (cache_length, place, keyvalue, key_cache[0], value_cache[0]),
        scalars=2,
    )
    (out,) = call(add_heads, [((OWN, FEATURES), BF16)], (collected,))
    return (out[None], new_key[None], new_value[None])


def solution(mesh):
    return jax.shard_map(
        body,
        mesh=mesh,
        in_specs=(
            P("gy", "gx", None),
            P(),
            P(),
            P("gy", "gx"),
            P("gy", "gx"),
            P("gx", "gy"),
            P("gy", "gx", None),
            P("gy", "gx", None),
            P("gy"),
        ),
        out_specs=(P("gy", "gx", None), P("gy", "gx", None), P("gy", "gx", None)),
        check_vma=False,
    )
```

```python
import jax
import jax.numpy as jnp
from jax import lax
from jax.experimental import pallas as pl
from jax.experimental.pallas import tpu as pltpu
from jax.sharding import PartitionSpec as P

CHIPS = 16
CORES = 2
LANES = 128
HALF = 64
PAGE = 72
OWN = 8
FEATURES = 2048
CHUNKS = FEATURES // LANES
KV_ROWS = 2 * PAGE
SEND_ROWS = KV_ROWS + OWN * CHUNKS
WEIGHT_ROWS = HALF + OWN
NEW = 256
NEGATIVE = -1e30

FIRST = 10
SAME_CORE = [[CORES * ((at + FIRST) % CHIPS) + core for at in range(CHIPS)] for core in range(CORES)]
COLUMNS = [
    [(CORES * chip + (odd + plane) % CORES) * CHUNKS + plane for plane in reversed(range(CHUNKS))]
    for chip in range(CHIPS)
    for odd in range(CORES)
]
ONE_CHIP = [[CORES * chip + core for core in range(CORES)] for chip in range(CHIPS)]
SWAP = [(place, place ^ 1) for place in range(CHIPS * CORES)]

F32 = jnp.float32
BF16 = jnp.bfloat16


def dot(a, b):
    return lax.dot_general(a, b, (((1,), (0,)), ((), ())), preferred_element_type=F32)


def dot_nt(a, b):
    return lax.dot_general(a, b, (((1,), (1,)), ((), ())), preferred_element_type=F32)


def iota(shape, dim):
    return lax.broadcasted_iota(jnp.int32, shape, dim)


def prepare(hidden, gain, bias, query_w, keyvalue_w, out_w, key_page, value_page, send, weights, *scratch):
    held, done = scratch[:-1], scratch[-1]
    targets = held + (
        weights.at[0:HALF],
        weights.at[HALF:WEIGHT_ROWS],
        weights.at[WEIGHT_ROWS : WEIGHT_ROWS + HALF],
    )
    sources = (hidden, gain, bias, key_page, value_page, query_w, keyvalue_w, out_w)
    copies = [
        pltpu.make_async_copy(source, target, done.at[at])
        for at, (source, target) in enumerate(zip(sources, targets))
    ]
    for copy in copies:
        copy.start()
    for copy in copies:
        copy.wait()
    values = held[0][...].astype(F32)
    average = jnp.mean(values, axis=-1, keepdims=True)
    centred = values - average
    spread = jnp.mean(centred * centred, axis=-1, keepdims=True)
    normed = (centred * lax.rsqrt(spread + 1e-05) * held[1][...] + held[2][...]).astype(BF16)
    key_rows = held[3][...]
    value_rows = held[4][...]
    for chip in range(CHIPS):
        send[chip, 0:PAGE, :] = key_rows
        send[chip, PAGE:KV_ROWS, :] = value_rows
        for chunk in range(CHUNKS):
            send[chip, KV_ROWS + OWN * chunk : KV_ROWS + OWN * (chunk + 1), :] = normed[
                :, LANES * chunk : LANES * (chunk + 1)
            ]


def part_of(gathered, odd, core, chunk):
    side = odd if (core + chunk) % CORES == 0 else 1 - odd
    return gathered.at[side, CHUNKS - 1 - chunk]


def gathered_tokens(tokens, chunks=range(CHUNKS)):
    pieces = []
    for chunk in chunks:
        first = KV_ROWS + OWN * chunk
        pieces.append(tokens[:, first : first + OWN, :].astype(F32).reshape(LANES, LANES).astype(BF16))
    return jnp.concatenate(pieces, axis=1)


def project_keyvalue(odd_ref, tokens, weights, planes, keyvalue, swapped):
    odd = odd_ref[0]
    narrow = jnp.concatenate(
        [
            jnp.concatenate(
                [part_of(weights, odd, core, chunk)[...].astype(F32) for core in range(CORES)], axis=0
            )
            for chunk in range(CHUNKS)
        ],
        axis=1,
    ).astype(BF16)
    rounded = dot_nt(narrow, gathered_tokens(tokens)).astype(BF16)
    for place in range(CHIPS * CORES):
        keyvalue[place] = rounded
    swapped[:, 0:KV_ROWS, :] = tokens[:, 0:KV_ROWS, :]
    swapped[:, KV_ROWS : KV_ROWS + HALF, :] = planes[:, WEIGHT_ROWS : WEIGHT_ROWS + HALF, :]
    swapped[:, KV_ROWS + HALF : SEND_ROWS, :] = planes[:, 0:HALF, :]


def project_queries(same, tokens, planes, peer):
    sums = []
    for parity in range(2):
        chunks = range(parity, CHUNKS, 2)
        square = jnp.concatenate(
            [
                jnp.concatenate(
                    [planes[CHUNKS - 1 - chunk, 0:HALF, :], peer[CHUNKS - 1 - chunk, KV_ROWS + HALF : SEND_ROWS, :]],
                    axis=0,
                )
                for chunk in chunks
            ],
            axis=1,
        )
        sums.append(dot_nt(gathered_tokens(tokens, chunks), square))
    total = sums[0] + pltpu.roll(sums[1], HALF, 1)
    return jnp.where(same, total, pltpu.roll(total, HALF, 1)).astype(BF16)


def new_columns(keyvalue, core, first):
    return jnp.concatenate([keyvalue[CORES * chip + core] for chip in range(first, first + CHIPS // 2)], axis=0)


def token_of(index, core):
    chip = ((index >> 3) + FIRST) & (CHIPS - 1)
    return (chip << 4) + OWN * core + (index & 7)


def attend_cached(
    length_ref, odd_ref, core_ref, own, planes, peer, queries, largest_out, total_out, summed_out
):
    length = length_ref[0]
    core = core_ref[0]
    scale = float(LANES) ** (-0.5)
    query_rows = project_queries((core + odd_ref[0]) % CORES == 0, own, planes, peer)
    queries[...] = query_rows
    places = CHIPS * PAGE
    lane = iota((1, places), 1)
    at = (lane * 911) >> 16
    chip = (at + FIRST) & (CHIPS - 1)
    start = lane - PAGE * at + KV_ROWS * chip
    scored = []
    value_sets = []
    for source, side in ((own, core), (peer, 1 - core)):
        key_rows = source[:, 0:PAGE, :].astype(F32).reshape(places, LANES).astype(BF16)
        value_sets.append(source[:, PAGE:KV_ROWS, :].astype(F32).reshape(places, LANES).astype(BF16))
        scores = dot_nt(query_rows, key_rows) * scale
        scored.append(jnp.where(start + PAGE * side < length, scores, NEGATIVE))
    largest = jnp.maximum(
        jnp.max(scored[0], axis=1, keepdims=True), jnp.max(scored[1], axis=1, keepdims=True)
    )
    total = jnp.zeros((LANES, 1), F32)
    summed = jnp.zeros((LANES, LANES), F32)
    for scores, value_rows in zip(scored, value_sets):
        terms = jnp.where(scores > 0.5 * NEGATIVE, jnp.exp(scores - largest), 0.0)
        total = total + jnp.sum(terms, axis=1, keepdims=True)
        summed = summed + dot(terms.astype(BF16), value_rows)
    largest_out[...] = jnp.broadcast_to(largest, (LANES, LANES))
    total_out[...] = jnp.broadcast_to(total, (LANES, LANES))
    summed_out[...] = summed


def attend_new(core_ref, odd_ref, queries, old_largest, old_total, old_summed, keyvalue, planes, peer, result):
    core = core_ref[0]
    scale = float(LANES) ** (-0.5)
    query_rows = queries[...]
    own_token = token_of(iota((LANES, LANES), 0), core)
    scored = []
    for side in range(CORES):
        scores = dot(query_rows, new_columns(keyvalue, side, 0)) * scale
        scored.append(jnp.where(token_of(iota((LANES, LANES), 1), side) <= own_token, scores, NEGATIVE))
    largest = jnp.max(jnp.maximum(scored[0], scored[1]), axis=1, keepdims=True)
    largest = jnp.maximum(old_largest[...], jnp.broadcast_to(largest, (LANES, LANES)))
    factor = jnp.exp(old_largest[...] - largest)
    terms = [jnp.exp(scores - largest) for scores in scored]
    total = old_total[...] * factor + jnp.sum(terms[0] + terms[1], axis=1, keepdims=True)
    summed = old_summed[...] * factor
    for side in range(CORES):
        summed = summed + dot_nt(terms[side].astype(BF16), new_columns(keyvalue, side, CHIPS // 2))
    attended = summed / total
    turned = pltpu.roll(attended, HALF, 1)
    same = (core + odd_ref[0]) % CORES == 0
    sides = (jnp.where(same, attended, turned).astype(BF16), jnp.where(same, turned, attended).astype(BF16))
    for parity in range(2):
        chunks = range(parity, CHUNKS, 2)
        wide = jnp.concatenate(
            [
                jnp.concatenate(
                    [
                        planes[CHUNKS - 1 - chunk, WEIGHT_ROWS : WEIGHT_ROWS + HALF, :],
                        peer[CHUNKS - 1 - chunk, KV_ROWS : KV_ROWS + HALF, :],
                    ],
                    axis=0,
                )
                for chunk in chunks
            ],
            axis=1,
        )
        part = dot(sides[parity], wide)
        for at, chunk in enumerate(chunks):
            result[:, OWN * chunk : OWN * (chunk + 1), :] = (
                part[:, LANES * at : LANES * (at + 1)].reshape(CHIPS, OWN, LANES).astype(BF16)
            )


def add_heads(parts, result):
    total = parts[0].astype(F32)
    for chip in range(1, CHIPS):
        total = total + parts[chip].astype(F32)
    for chunk in range(CHUNKS):
        result[:, LANES * chunk : LANES * (chunk + 1)] = total[OWN * chunk : OWN * (chunk + 1), :].astype(BF16)


def write_pages(length_ref, place_ref, keyvalue, key_page, value_page, new_key, new_value):
    length = length_ref[0]
    base = place_ref[0] * PAGE - length
    offset = iota((PAGE, LANES), 0) + base
    inside = (offset >= 0) & (offset < NEW)
    key_rows = jnp.zeros((PAGE, LANES), F32)
    value_rows = jnp.zeros((PAGE, LANES), F32)
    for side in range(CORES):
        chosen = (offset == token_of(iota((PAGE, LANES), 1), side)).astype(F32).astype(BF16)
        key_rows = key_rows + dot_nt(chosen, new_columns(keyvalue, side, 0))
        value_rows = value_rows + dot_nt(chosen, new_columns(keyvalue, side, CHIPS // 2))
    new_key[...] = jnp.where(inside, key_rows, key_page[...].astype(F32)).astype(BF16)
    new_value[...] = jnp.where(inside, value_rows, value_page[...].astype(F32)).astype(BF16)


def call(kernel, shapes, arguments, scalars=0, held=None):
    space = pltpu.VMEM if held is None else pltpu.HBM
    specs = [
        pl.BlockSpec(memory_space=pltpu.SMEM if at < scalars else space) for at in range(len(arguments))
    ]
    scratch = []
    if held is not None:
        scratch = [pltpu.VMEM(shape, dtype) for shape, dtype in held]
        scratch.append(pltpu.SemaphoreType.DMA((len(arguments),)))
    if held is not None:
        arguments = [pltpu.with_memory_space_constraint(argument, pltpu.HBM) for argument in arguments]
    return pl.pallas_call(
        kernel,
        out_shape=[jax.ShapeDtypeStruct(shape, dtype) for shape, dtype in shapes],
        in_specs=specs,
        out_specs=[pl.BlockSpec(memory_space=pltpu.VMEM)] * len(shapes),
        scratch_shapes=scratch,
        compiler_params=pltpu.CompilerParams(vmem_limit_bytes=48 * 1024 * 1024),
    )(*arguments)


def body(
    hidden_states,
    norm_gain,
    norm_bias,
    query_weight,
    keyvalue_weight,
    out_weight,
    key_cache,
    value_cache,
    cache_length,
):
    place = lax.axis_index("gx").astype(jnp.int32).reshape(1)
    core = place & 1
    odd = lax.axis_index("gy").astype(jnp.int32).reshape(1) & 1
    send, weights = call(
        prepare,
        [((CHIPS, SEND_ROWS, LANES), BF16), ((WEIGHT_ROWS + HALF, LANES), BF16)],
        (
            hidden_states[0],
            norm_gain.reshape(1, FEATURES),
            norm_bias.reshape(1, FEATURES),
            query_weight.T,
            keyvalue_weight.T,
            out_weight,
            key_cache[0],
            value_cache[0],
        ),
        held=[
            ((OWN, FEATURES), BF16),
            ((1, FEATURES), F32),
            ((1, FEATURES), F32),
            ((PAGE, LANES), BF16),
            ((PAGE, LANES), BF16),
        ],
    )
    own = lax.all_to_all(send, "gx", 0, 0, tiled=True, axis_index_groups=SAME_CORE)
    planes = lax.all_gather(weights, ("gx", "gy"), axis=0, tiled=False, axis_index_groups=COLUMNS)
    own, planes = lax.optimization_barrier((own, planes))
    inner = lax.all_gather(planes[:, HALF:WEIGHT_ROWS], "gx", axis=0, tiled=False, axis_index_groups=ONE_CHIP)
    rows, swapped = call(
        project_keyvalue,
        [((CHIPS * CORES, CORES * OWN, LANES), BF16), ((CHIPS, SEND_ROWS, LANES), BF16)],
        (odd, own, inner, planes),
        scalars=1,
    )
    keyvalue = lax.all_to_all(rows, "gx", 0, 0, tiled=True)
    peer = lax.ppermute(swapped, "gx", SWAP)
    queries, largest, total, summed = call(
        attend_cached,
        [((LANES, LANES), BF16)] + [((LANES, LANES), F32)] * 3,
        (cache_length, odd, core, own, planes, peer),
        scalars=3,
    )
    (parts,) = call(
        attend_new,
        [((CHIPS, LANES, LANES), BF16)],
        (core, odd, queries, largest, total, summed, keyvalue, planes, peer),
        scalars=2,
    )
    collected = lax.all_to_all(parts, "gx", 0, 0, tiled=True, axis_index_groups=SAME_CORE)
    new_key, new_value = call(
        write_pages,
        [((PAGE, LANES), BF16), ((PAGE, LANES), BF16)],
        (cache_length, place, keyvalue, key_cache[0], value_cache[0]),
        scalars=2,
    )
    (out,) = call(add_heads, [((OWN, FEATURES), BF16)], (collected,))
    return (out[None], new_key[None], new_value[None])


def solution(mesh):
    return jax.shard_map(
        body,
        mesh=mesh,
        in_specs=(
            P("gy", "gx", None),
            P(),
            P(),
            P("gy", "gx"),
            P("gy", "gx"),
            P("gx", "gy"),
            P("gy", "gx", None),
            P("gy", "gx", None),
            P("gy"),
        ),
        out_specs=(P("gy", "gx", None), P("gy", "gx", None), P("gy", "gx", None)),
        check_vma=False,
    )
```
